32 devices in a mesh: heads: 4 (over x, core), seq: 8 (over z, y).
Axes of the slice: x: 2, y: 2, z: 4, core: 2. Of those that a mesh axis runs over, the one named last changes fastest.
Arguments:
- tokens: bfloat16 [2048, 4096], P('seq'), may hold values from -6 to 6
- norm_gain: float32 [4096], replicated, may hold values from 0.1 to 1.9
- w_query: bfloat16 [4096, 4096], P(None, 'heads'), may hold values from -0.09375 to 0.09375
- w_key: bfloat16 [4096, 1024], P(None, 'heads'), may hold values from -0.1875 to 0.1875
- w_value: bfloat16 [4096, 1024], P(None, 'heads'), may hold values from -0.375 to 0.375
- w_out: bfloat16 [4096, 4096], P('heads'), may hold values from -0.09375 to 0.09375
- cache_keys: bfloat16 [8, 8192, 128], P('heads', 'seq'), may hold values from -360 to 360
- cache_values: bfloat16 [8, 8192, 128], P('heads', 'seq'), may hold values from -24 to 24
- vert_blocks: int32 [8, 64], P('heads'), may hold values from -1 to 127, as said below
- vert_count: int32 [8], P('heads'), may hold values from 32 to 64
- slash_offsets: int32 [8, 4], P('heads'), may hold values from -1 to 4, as said below
- slash_count: int32 [8], P('heads'), may hold values from 1 to 4
Outputs:
- layer_out: bfloat16 [2048, 4096], P('seq', 'heads')
The draws below stay inside these ranges and needn't reach their ends.
Inputs may be any that keep to these rules, and one draw needn't show every extreme that they name: `vert_blocks`: row g lists cache blocks for key/value head g: its entries before vert_count[g] are distinct, the rest are -1. The cache of one index of seq holds at most 8 of the blocks that a row lists, and exactly 8 for one index in every row. `slash_offsets`: entries of row g before slash_count[g] are distinct, the rest are -1.
All inputs are finite; a program needn't handle non-finite values.
Results may differ from the reference program's by a relative error of at most 0.015.
The reference program's roundings to bfloat16 on the way count: a program that leaves them out, or rounds other values in their place, can miss the bound.
Values may be sent and summed in bfloat16 or wider, within the bound.
A program may use at most 64 MiB of HBM per device.

```python
import math
import jax
import jax.numpy as jnp
from jax import lax

D = 4096
QH = 32
KVH = 8
HD = 128
BLK = 64
NV = 64
VCAP = 8
SMAX = 4
CACHE_DEV = 1024
TOKENS = 2048
CACHE = 8192


def vertical_lists(key):
    base_key = jax.random.fold_in(key, 7)
    count_key, pick_key, hot_key, order_key, tie_key, mix_key = jax.random.split(base_key, 6)
    device_total = CACHE // CACHE_DEV
    per_device = CACHE_DEV // BLK
    counts = jax.random.randint(count_key, (KVH,), NV // 2, NV + 1)
    chosen_heads = jax.random.permutation(pick_key, KVH)
    counts = counts.at[chosen_heads[0]].set(NV).at[chosen_heads[1]].set(NV // 2)
    hot_device = jax.random.randint(hot_key, (KVH,), 0, device_total)
    order_scores = jax.random.randint(order_key, (KVH, device_total, per_device), 0, 2 ** 16) * per_device + jnp.arange(per_device)
    block_order = jnp.argsort(order_scores, axis=-1, stable=True)[:, :, :VCAP]
    candidate = jnp.arange(device_total)[None, :, None] * per_device + block_order
    hot_device_mask = jnp.arange(device_total)[None, :] == hot_device[:, None]
    priority = jnp.where(hot_device_mask[:, :, None], 0, 1 + jnp.arange(VCAP)[None, None, :])
    tie_break = jax.random.randint(tie_key, (KVH, device_total, VCAP), 0, 1024)
    flat_index = jnp.arange(device_total * VCAP).reshape(device_total, VCAP)[None]
    ranking = (priority * 1024 + tie_break) * (device_total * VCAP) + flat_index
    pick_order = jnp.argsort(ranking.reshape(KVH, -1), axis=-1, stable=True)[:, :NV]
    picked = jnp.take_along_axis(candidate.reshape(KVH, -1), pick_order, axis=1)
    positions = jnp.arange(NV)[None, :]
    live_entry = positions < counts[:, None]
    mixing = jnp.where(live_entry, jax.random.randint(mix_key, (KVH, NV), 0, 2 ** 12) * NV + positions, 2 ** 22 + positions)
    shuffle = jnp.argsort(mixing, axis=-1, stable=True)
    block_lists = jnp.take_along_axis(picked, shuffle, axis=1)
    return (jnp.where(live_entry, block_lists, -1).astype(jnp.int32), counts.astype(jnp.int32))


def slash_lists(key):
    base_key = jax.random.fold_in(key, 11)
    count_key, pick_key, order_key = jax.random.split(base_key, 3)
    counts = jax.random.randint(count_key, (KVH,), 1, SMAX + 1)
    chosen_heads = jax.random.permutation(pick_key, KVH)
    counts = counts.at[chosen_heads[0]].set(SMAX).at[chosen_heads[1]].set(1)
    scores = jax.random.randint(order_key, (KVH, SMAX), 0, 2 ** 16) * SMAX + jnp.arange(SMAX)
    offsets = jnp.argsort(scores, axis=-1, stable=True) + 1
    live_entry = jnp.arange(SMAX)[None, :] < counts[:, None]
    return (jnp.where(live_entry, offsets, -1).astype(jnp.int32), counts.astype(jnp.int32))


def draw_vert_blocks(key, part):
    return vertical_lists(key)[0]


def draw_vert_count(key, part):
    return vertical_lists(key)[1]


def draw_slash_offsets(key, part):
    return slash_lists(key)[0]


def draw_slash_count(key, part):
    return slash_lists(key)[1]


def draw_cache_keys(key, part):
    noise_key = jax.random.fold_in(jax.random.fold_in(key, 3), 0)
    values = jnp.clip(jax.random.normal(noise_key, (KVH, CACHE, HD), jnp.float32), -6.0, 6.0) * 2.0
    return values.astype(jnp.bfloat16)


def block_levels(own_key, shape, pieces, least, largest):
    level = 1.0
    for dim, shards_of in pieces:
        draws = jax.random.uniform(jax.random.fold_in(jax.random.fold_in(own_key, 6), dim), (shards_of,), jnp.float32, least / len(pieces), largest / len(pieces))
        level = level * jnp.repeat(jnp.exp(draws), shape[dim] // shards_of).reshape((-1,) + (1,) * (len(shape) - 1 - dim))
    return level


def noise(rng, shape, deviation, limit, pieces=(), held_as=jnp.bfloat16):
    drawn = jax.random.normal(rng, shape, jnp.float32) * deviation
    if len(pieces) > 0:
        drawn = block_levels(rng, shape, pieces, -0.22, 0.18) * drawn
    return jnp.clip(drawn, min=-limit, max=limit).astype(held_as)


def setup_inputs(seed: int = 0) -> dict:
    key_list = jax.random.split(jax.random.key(seed), 13)
    return {
        "tokens": noise(key_list[0], (TOKENS, D), 1.0, 6.0, ((0, 8),)),
        "norm_gain": jnp.clip(1.0 + 0.18 * jax.random.normal(key_list[1], (D,), jnp.float32), 0.1, 1.9),
        "w_query": noise(key_list[2], (D, QH * HD), D ** -0.5, 0.09375, ((1, 4),)),
        "w_key": noise(key_list[3], (D, KVH * HD), (D // 4) ** -0.5, 0.1875, ((1, 4),)),
        "w_value": noise(key_list[4], (D, KVH * HD), (D // 16) ** -0.5, 0.375, ((1, 4),)),
        "w_out": noise(key_list[5], (QH * HD, D), (QH * HD) ** -0.5, 0.09375, ((0, 4),)),
        "cache_keys": draw_cache_keys(jax.random.fold_in(key_list[12], 71), 0),
        "cache_values": noise(key_list[7], (KVH, CACHE, HD), 4.0, 24.0, ((0, 4), (1, 8))),
        "vert_blocks": draw_vert_blocks(jax.random.fold_in(key_list[12], 71), 0),
        "vert_count": draw_vert_count(jax.random.fold_in(key_list[12], 71), 0),
        "slash_offsets": draw_slash_offsets(jax.random.fold_in(key_list[12], 71), 0),
        "slash_count": draw_slash_count(jax.random.fold_in(key_list[12], 71), 0),
    }


def reference(tokens, norm_gain, w_query, w_key, w_value, w_out, cache_keys, cache_values, vert_blocks, vert_count, slash_offsets, slash_count):
    activation = tokens.astype(jnp.float32)
    normed = (activation * lax.rsqrt(lax.optimization_barrier(jnp.mean(activation * activation, axis=-1, keepdims=True)) + 1e-05) * norm_gain).astype(jnp.bfloat16)
    queries = jnp.dot(normed, w_query, preferred_element_type=jnp.float32).astype(jnp.bfloat16)
    key_rows = jnp.dot(normed, w_key, preferred_element_type=jnp.float32).astype(jnp.bfloat16)
    value_rows = jnp.dot(normed, w_value, preferred_element_type=jnp.float32).astype(jnp.bfloat16)
    group_size = QH // KVH
    score_scale = 1.0 / math.sqrt(HD)
    query_blocks = TOKENS // BLK
    head_queries = queries.reshape(TOKENS, QH, HD).transpose(1, 0, 2)
    new_keys = key_rows.reshape(TOKENS, KVH, HD).transpose(1, 0, 2).reshape(KVH, query_blocks, BLK, HD)
    new_values = value_rows.reshape(TOKENS, KVH, HD).transpose(1, 0, 2).reshape(KVH, query_blocks, BLK, HD)
    cache_key_blocks = cache_keys.reshape(KVH, CACHE // BLK, BLK, HD)
    cache_value_blocks = cache_values.reshape(KVH, CACHE // BLK, BLK, HD)
    offsets_all = jnp.arange(SMAX + 1)
    inner_row = jnp.arange(BLK)

    def one_head(head_index):
        shared_head = head_index // group_size
        query_rows = head_queries[head_index]
        live_entry = jnp.arange(NV) < vert_count[shared_head]
        picked = jnp.clip(vert_blocks[shared_head], 0, CACHE // BLK - 1)
        far_keys = jnp.take(cache_key_blocks[shared_head], picked, axis=0).reshape(NV * BLK, HD)
        far_values = jnp.take(cache_value_blocks[shared_head], picked, axis=0).reshape(NV * BLK, HD)
        far_scores = jnp.dot(query_rows, far_keys.T, preferred_element_type=jnp.float32) * score_scale
        far_scores = jnp.where(jnp.repeat(live_entry, BLK)[None, :], far_scores, -jnp.inf)
        padded_keys = jnp.concatenate([jnp.zeros((SMAX, BLK, HD), jnp.bfloat16), new_keys[shared_head]], 0)
        padded_values = jnp.concatenate([jnp.zeros((SMAX, BLK, HD), jnp.bfloat16), new_values[shared_head]], 0)
        window_keys = jnp.stack([padded_keys[SMAX - offset:SMAX - offset + query_blocks] for offset in range(SMAX + 1)], 0)
        window_values = jnp.stack([padded_values[SMAX - offset:SMAX - offset + query_blocks] for offset in range(SMAX + 1)], 0)
        blocked_queries = query_rows.reshape(query_blocks, BLK, HD).astype(jnp.float32)
        near_scores = jnp.einsum('bih,objh->bioj', blocked_queries, window_keys.astype(jnp.float32)) * score_scale
        slash_hit = jnp.any((slash_offsets[shared_head][None, :] == offsets_all[:, None]) & (jnp.arange(SMAX)[None, :] < slash_count[shared_head]), axis=1)
        exists = jnp.arange(query_blocks)[:, None] - offsets_all[None, :] >= 0
        causal = inner_row[:, None] >= inner_row[None, :]
        allowed = exists[:, None, :, None] & (slash_hit[None, None, :, None] | (offsets_all == 0)[None, None, :, None] & causal[None, :, None, :])
        near_scores = jnp.where(allowed, near_scores, -jnp.inf).reshape(TOKENS, (SMAX + 1) * BLK)
        row_max = jnp.maximum(lax.optimization_barrier(jnp.max(far_scores, axis=1)), lax.optimization_barrier(jnp.max(near_scores, axis=1)))
        far_weights = jnp.exp(far_scores - row_max[:, None])
        near_weights = jnp.exp(near_scores - row_max[:, None])
        weight_sum = lax.optimization_barrier(jnp.sum(far_weights, axis=1)) + lax.optimization_barrier(jnp.sum(near_weights, axis=1))
        mixed_out = jnp.dot(far_weights.astype(jnp.bfloat16), far_values, preferred_element_type=jnp.float32)
        near_rounded = near_weights.astype(jnp.bfloat16).astype(jnp.float32).reshape(query_blocks, BLK, SMAX + 1, BLK)
        mixed_out = mixed_out + jnp.einsum('bioj,objh->bih', near_rounded, window_values.astype(jnp.float32)).reshape(TOKENS, HD)
        return (mixed_out / weight_sum[:, None]).astype(jnp.bfloat16)
    attended = lax.map(one_head, jnp.arange(QH))
    attended = attended.transpose(1, 0, 2).reshape(TOKENS, QH * HD)
    return jnp.dot(attended, w_out, preferred_element_type=jnp.float32).astype(jnp.bfloat16)
```

```python
import functools
import math

import jax
import jax.numpy as jnp
from jax import lax
from jax.experimental import pallas as pl
from jax.experimental.pallas import tpu as pltpu
from jax.sharding import PartitionSpec as P

BLK = 64
VCAP = 8
SMAX = 4
MESH = pl.DeviceIdType.MESH


def pick_kernel(vb, vc, ck, cv, kv, table, sems):
    heads, per_device = ck.shape[0], ck.shape[1] // BLK
    first = lax.axis_index("seq") * per_device
    stride = 2 * VCAP

    def copies(g, r, row):
        return [
            pltpu.make_async_copy(
                src.at[g, pl.ds(row, BLK)], kv.at[g, j, pl.ds(r * BLK, BLK)], sems.at[g, j, r]
            )
            for j, src in enumerate((ck, cv))
        ]

    for g in range(heads):
        count = jnp.int32(0)
        live = vc[g]
        for e in range(vb.shape[1]):
            block = vb[g, e] - first
            table[g * stride + count] = block
            mine = (e < live) & (block >= 0) & (block < per_device)
            count = count + mine.astype(jnp.int32)
        spare = jnp.where(count > 0, table[g * stride], 0)
        for r in range(VCAP):
            block = jnp.where(r < count, table[g * stride + r], spare)
            for copy in copies(g, r, pl.multiple_of(block * BLK, BLK)):
                copy.start()
    for g in range(heads):
        for r in range(VCAP):
            for copy in copies(g, r, 0):
                copy.wait()


def layer_kernel(
    n,
    chips,
    per_device,
    vc,
    so,
    sc,
    vb,
    gain,
    tok_hbm,
    wq_hbm,
    wk_hbm,
    wv_hbm,
    wo_hbm,
    kv_hbm,
    out,
    tok,
    normed,
    wq,
    wk,
    wv,
    wo,
    kv,
    near,
    prev,
    q,
    acc,
    mx,
    owner,
    att,
    core_out,
    core_in,
    x_out,
    x_in,
    part,
    load_sem,
    own_sem,
    send_sem,
    recv_sem,
    near_send,
    near_recv,
    core_send,
    core_recv,
    x_send,
    x_recv,
):
    head = lax.axis_index("heads")
    seq = lax.axis_index("seq")
    col, row = lax.rem(seq, 2), lax.div(seq, 2)
    other = 1 - col
    length = n // 2
    groups = kv.shape[1]
    hd, rows = q.shape[2], acc.shape[2]
    qheads = acc.shape[0]
    per = qheads // groups
    mate = row + 1 - 2 * lax.rem(row, 2)
    up = mate > row
    core_peer = head + 1 - 2 * lax.rem(head, 2)
    span_heads = 2 * chips

    def chip_peer(h, step):
        return lax.rem(h + 2 * step, span_heads)

    tile = wq.shape[1] // 4

    loads = [
        pltpu.make_async_copy(tok_hbm, tok, load_sem.at[0]),
        pltpu.make_async_copy(wk_hbm, wk, load_sem.at[1]),
        pltpu.make_async_copy(wv_hbm, wv, load_sem.at[2]),
    ]
    for j in range(4):
        cols = pl.ds(j * tile, tile)
        loads.append(pltpu.make_async_copy(wq_hbm.at[:, cols], wq.at[:, cols], load_sem.at[3 + j]))
    loads.append(pltpu.make_async_copy(wo_hbm, wo, load_sem.at[7]))
    own = pltpu.make_async_copy(kv_hbm, kv.at[seq], own_sem)
    own.start()
    for copy in loads[:4]:
        copy.start()

    barrier = pltpu.get_barrier_semaphore()

    def greet(h, s):
        pl.semaphore_signal(barrier, inc=1, device_id=(h, s), device_id_type=MESH)

    greet(core_peer, seq)
    for step in range(1, chips):
        greet(chip_peer(head, step), seq)
    greet(head, row * 2 + other)

    @pl.when(row > 0)
    def _():
        greet(head, seq - 2)

    @pl.when(row < length - 1)
    def _():
        greet(head, seq + 2)

    @pl.when(seq > 0)
    def _():
        greet(head, seq - 1)

    @pl.when(seq < n - 1)
    def _():
        greet(head, seq + 1)

    def flag(c):
        return jnp.where(c, 1, 0)

    pl.semaphore_wait(
        barrier,
        chips + 1 + flag(row > 0) + flag(row < length - 1) + flag(seq > 0) + flag(seq < n - 1),
    )

    def hop(s, g, way, src=None):
        target = (seq + 2, seq - 2, row * 2 + other)[way]
        return pltpu.make_async_remote_copy(
            src_ref=kv.at[s, g] if src is None else src.at[g],
            dst_ref=kv.at[s, g],
            send_sem=send_sem.at[way, s, g],
            recv_sem=recv_sem.at[s, g],
            device_id=(head, target),
            device_id_type=MESH,
        )

    for g in range(groups):

        @pl.when(row < length - 1)
        def _():
            hop(seq, g, 0, kv_hbm).start()

        @pl.when(row > 0)
        def _():
            hop(seq, g, 1, kv_hbm).start()

        hop(seq, g, 2, kv_hbm).start()

    loads[0].wait()
    for copy in loads[4:]:
        copy.start()

    @pl.loop(0, rows // 32)
    def _(i):
        span = pl.ds(pl.multiple_of(i * 32, 32), 32)
        a = tok[span, :].astype(jnp.float32)
        scale = lax.rsqrt(jnp.mean(a * a, axis=-1, keepdims=True) + 1e-05)
        normed[span, :] = (a * scale * gain[...]).astype(jnp.bfloat16)

    for j, w in enumerate((wk, wv)):
        loads[1 + j].wait()
        res = jnp.dot(normed[...], w[...], preferred_element_type=jnp.float32).astype(jnp.bfloat16)
        for g in range(groups):
            near[g, j] = res[:, g * hd : (g + 1) * hd]

    for j in range(4):
        loads[3 + j].wait()
        res = jnp.dot(
            normed[...], wq[:, j * tile : (j + 1) * tile], preferred_element_type=jnp.float32
        ).astype(jnp.bfloat16)
        for k in range(tile // hd):
            q[j * (tile // hd) + k] = res[:, k * hd : (k + 1) * hd]
        if j == 0:
            shift = pltpu.make_async_remote_copy(
                src_ref=near,
                dst_ref=prev,
                send_sem=near_send,
                recv_sem=near_recv,
                device_id=(head, jnp.where(seq < n - 1, seq + 1, seq - 1)),
                device_id_type=MESH,
            )

            @pl.when(seq < n - 1)
            def _():
                shift.start()

    def reach(t, d):
        r = row + t * (2 * d - 1)
        return r, (r >= 0) & (r < length)

    def across(r, g):
        return (r != mate) | (g < groups - 1)

    def relay(t):
        for g in range(groups):
            for d in range(2):
                r, ok = reach(t, d)

                @pl.when(ok)
                def _():
                    s = r * 2 + col
                    hop(s, g, 2).wait_recv()

                    @pl.when((row > 0) if d else (row < length - 1))
                    def _():
                        hop(s, g, 1 if d else 0).start()

                    @pl.when(across(r, g))
                    def _():
                        hop(s, g, 2).start()

    relay(1)

    factor = math.log2(math.e) / math.sqrt(hd)

    extra = acc.shape[1] - hd

    def fold(g, keys, values, allowed=None, live=None, some=None):
        heads = [g * per + k for k in range(per)]
        old = [(mx[h], acc[h]) for h in heads]
        fresh = []
        ones = jnp.ones((extra, keys.shape[0]), jnp.bfloat16)
        lhs = jnp.concatenate([jnp.transpose(values), ones], axis=0)
        if live is not None:
            lhs = lhs * live

        def score(h):
            res = lax.dot_general(
                keys, q[h], (((1,), (1,)), ((), ())), preferred_element_type=jnp.float32
            )
            return res if allowed is None else jnp.where(allowed, res, -jnp.inf)

        ahead = score(heads[0])
        for k, (m, a) in enumerate(old):
            scores = ahead
            if k + 1 < per:
                ahead = score(heads[k + 1])
            new = jnp.maximum(m, jnp.max(scores, axis=0, keepdims=True))
            weights = jnp.exp2((scores - new) * factor).astype(jnp.bfloat16)
            if some is not None:
                new = jnp.where(some, new, m)
            decay = jnp.exp2((m - new) * factor)
            a = a * decay + jnp.dot(lhs, weights, preferred_element_type=jnp.float32)
            fresh.append((new, a))
        for h, (m, a) in zip(heads, fresh):
            mx[h], acc[h] = m, a

    shape = (rows, rows)
    u_index = lax.broadcasted_iota(jnp.int32, shape, 0)
    t_index = lax.broadcasted_iota(jnp.int32, shape, 1)
    gap = t_index // BLK - u_index // BLK
    mx[...] = jnp.full(mx.shape, -1e30, jnp.float32)
    acc[...] = jnp.zeros(acc.shape, jnp.float32)

    def spans(g, rows_ref, offset):
        allowed = (gap + offset == 0) & (u_index <= t_index)
        for e in range(so.shape[1]):
            step = jnp.where(e < sc[g], so[g, e], -1)
            allowed = allowed | ((gap + offset == step) & (step >= 0))
        fold(g, rows_ref[g, 0], rows_ref[g, 1], allowed)
        return 0

    lax.fori_loop(0, groups, lambda g, _: spans(g, near, 0), 0)

    slots = kv.shape[3]
    slot_block = lax.broadcasted_iota(jnp.int32, (extra, slots), 1) // BLK
    slot_block = slot_block.astype(jnp.float32)
    entry = lax.broadcasted_iota(jnp.int32, (1, vb.shape[1]), 1)
    for g in range(groups):
        block = vb[g : g + 1, :]
        owner[g] = jnp.where((entry < vc[g]) & (block >= 0), lax.div(block, per_device), -1)

    def attend(s, g):
        held = jnp.where(owner[g] == s, 1.0, 0.0)
        count = jnp.sum(held, axis=1, keepdims=True)
        live = jnp.where(slot_block < count, 1.0, 0.0).astype(jnp.bfloat16)
        live = jnp.concatenate([live] * (acc.shape[1] // extra), axis=0)
        fold(g, kv[s, g, 0], kv[s, g, 1], live=live, some=count > 0)

    own.wait()

    def own_shard(g, _):
        attend(seq, g)
        return 0

    lax.fori_loop(0, groups, own_shard, 0)

    def visit(t, side, wait):
        def one(i, _):
            g, d = lax.div(i, 2), lax.rem(i, 2)
            r, ok = reach(t, d)
            if wait:
                ok = ok & ((t > 0) | (d == 0)) & across(r, g)

            @pl.when(ok)
            def _():
                s = r * 2 + side
                if wait:
                    hop(s, g, 2).wait_recv()
                attend(s, g)

            return 0

        lax.fori_loop(0, 2 * groups, one, 0)

    def rounds(t, _):
        visit(t, col, False)

        @pl.when(t < length - 1)
        def _():
            relay(t + 1)

        visit(t - 1, other, True)

        @pl.when((t == 1) & (seq > 0))
        def _():
            shift.wait_recv()
            lax.fori_loop(0, groups, lambda g, _: spans(g, prev, rows // BLK), 0)

        @pl.when((t == max(length - 2, 1)) & up)
        def _():
            hop(row * 2 + other, groups - 1, 0).start()

        @pl.when((t == max(length - 2, 1)) & jnp.logical_not(up))
        def _():
            hop(row * 2 + other, groups - 1, 1).start()

        return 0

    lax.fori_loop(1, length + 1, rounds, 0)
    last = mate * 2 + other
    hop(last, groups - 1, 2).wait_recv()
    attend(last, groups - 1)

    for h in range(qheads):
        att[:, h * hd : (h + 1) * hd] = jnp.transpose(acc[h, :hd] / acc[h, hd : hd + 1]).astype(jnp.bfloat16)

    loads[7].wait()
    width = part.shape[2]
    pieces = out.shape[1] // width

    def product(target, j):
        start = pl.multiple_of(target * out.shape[1] + j * width, width)
        return jnp.dot(att[...], wo[:, pl.ds(start, width)], preferred_element_type=jnp.float32)

    def core_copy(i):
        return pltpu.make_async_remote_copy(
            src_ref=core_out.at[i],
            dst_ref=core_in.at[i],
            send_sem=core_send.at[i],
            recv_sem=core_recv.at[i],
            device_id=(core_peer, seq),
            device_id_type=MESH,
        )

    def x_copy(step, j):
        i = (step - 1) * pieces + j
        return pltpu.make_async_remote_copy(
            src_ref=x_out.at[i],
            dst_ref=x_in.at[i],
            send_sem=x_send.at[i],
            recv_sem=x_recv.at[i],
            device_id=(chip_peer(head, step), seq),
            device_id_type=MESH,
        )

    todo = [(step, j) for step in range(1, chips + 1) for j in range(pieces)]

    def exchange(i):
        step, j = todo[i]
        core_out[i] = product(chip_peer(core_peer, step), j).astype(jnp.bfloat16)
        core_copy(i).start()
        part[i] = product(chip_peer(head, step), j)

    def combine(i):
        step, j = todo[i]
        core_copy(i).wait_recv()
        both = part[i] + core_in[i].astype(jnp.float32)
        if step < chips:
            x_out[i] = both.astype(jnp.bfloat16)
        else:
            part[i] = both

    def forward(i):
        combine(i)
        if todo[i][0] < chips:
            x_copy(*todo[i]).start()

    lag = min(2, len(todo))
    for i in range(len(todo)):
        exchange(i)
        if i >= lag:
            forward(i - lag)
    for i in range(len(todo) - lag, len(todo)):
        forward(i)
    for j in range(pieces):
        total = part[len(todo) - pieces + j]
        for step in range(1, chips):
            x_copy(step, j).wait_recv()
            total = total + x_in[(step - 1) * pieces + j].astype(jnp.float32)
        out[:, j * width : (j + 1) * width] = total.astype(jnp.bfloat16)
    for i, (step, j) in enumerate(todo):
        core_copy(i).wait_send()
        if step < chips:
            x_copy(step, j).wait_send()

    @pl.when(seq < n - 1)
    def _():
        shift.wait_send()

    def settle(t, _):
        for g in range(groups):
            for d in range(2):
                r, ok = reach(t, d)
                once = ok if d else ok & (t > 0)

                @pl.when(once)
                def _():
                    s = r * 2 + col

                    @pl.when(across(r, g))
                    def _():
                        hop(s, g, 2).wait_send()

                    @pl.when((row > 0) & ((t == 0) | (d == 1)))
                    def _():
                        hop(s, g, 1).wait_send()

                    @pl.when((row < length - 1) & ((t == 0) | (d == 0)))
                    def _():
                        hop(s, g, 0).wait_send()

        return 0

    lax.fori_loop(0, length, settle, 0)

    @pl.when(up)
    def _():
        hop(row * 2 + other, groups - 1, 0).wait_send()

    @pl.when(jnp.logical_not(up))
    def _():
        hop(row * 2 + other, groups - 1, 1).wait_send()


def local(
    n,
    chips,
    tokens,
    norm_gain,
    w_query,
    w_key,
    w_value,
    w_out,
    cache_keys,
    cache_values,
    vert_blocks,
    vert_count,
    slash_offsets,
    slash_count,
):
    groups, _, hd = cache_keys.shape
    rows, model = tokens.shape
    qcols = w_query.shape[1]
    qheads = qcols // hd
    out_cols = w_out.shape[1] // (2 * chips)
    slots = VCAP * BLK
    bf16, f32 = jnp.bfloat16, jnp.float32
    smem = pl.BlockSpec(memory_space=pltpu.SMEM)
    vmem = pl.BlockSpec(memory_space=pltpu.VMEM)
    hbm = pl.BlockSpec(memory_space=pl.ANY)
    kv = pl.pallas_call(
        pick_kernel,
        out_shape=jax.ShapeDtypeStruct((groups, 2, slots, hd), bf16),
        in_specs=[smem] * 2 + [hbm] * 2,
        out_specs=hbm,
        scratch_shapes=[
            pltpu.SMEM((groups * 2 * VCAP,), jnp.int32),
            pltpu.SemaphoreType.DMA((groups, 2, VCAP)),
        ],
        compiler_params=pltpu.CompilerParams(vmem_limit_bytes=60 << 20),
        name="pick",
    )(vert_blocks, vert_count, cache_keys, cache_values)
    pieces = 4
    width = out_cols // pieces
    dma = pltpu.SemaphoreType.DMA
    return pl.pallas_call(
        functools.partial(layer_kernel, n, chips, cache_keys.shape[1] // BLK),
        out_shape=jax.ShapeDtypeStruct((rows, out_cols), bf16),
        in_specs=[smem] * 3 + [vmem] * 2 + [hbm] * 6,
        out_specs=vmem,
        scratch_shapes=[
            pltpu.VMEM((rows, model), bf16),
            pltpu.VMEM((rows, model), bf16),
            pltpu.VMEM(w_query.shape, bf16),
            pltpu.VMEM(w_key.shape, bf16),
            pltpu.VMEM(w_value.shape, bf16),
            pltpu.VMEM(w_out.shape, bf16),
            pltpu.VMEM((n, groups, 2, slots, hd), bf16),
            pltpu.VMEM((groups, 2, rows, hd), bf16),
            pltpu.VMEM((groups, 2, rows, hd), bf16),
            pltpu.VMEM((qheads, rows, hd), bf16),
            pltpu.VMEM((qheads, hd + 16, rows), f32),
            pltpu.VMEM((qheads, 1, rows), f32),
            pltpu.VMEM((groups, 1, vert_blocks.shape[1]), jnp.int32),
            pltpu.VMEM((rows, qcols), bf16),
            pltpu.VMEM((chips * pieces, rows, width), bf16),
            pltpu.VMEM((chips * pieces, rows, width), bf16),
            pltpu.VMEM(((chips - 1) * pieces, rows, width), bf16),
            pltpu.VMEM(((chips - 1) * pieces, rows, width), bf16),
            pltpu.VMEM((chips * pieces, rows, width), f32),
            dma((8,)),
            dma(()),
            dma((3, n, groups)),
            dma((n, groups)),
            dma(()),
            dma(()),
            dma((chips * pieces,)),
            dma((chips * pieces,)),
            dma(((chips - 1) * pieces,)),
            dma(((chips - 1) * pieces,)),
        ],
        compiler_params=pltpu.CompilerParams(
            collective_id=0, has_side_effects=True, vmem_limit_bytes=60 << 20
        ),
        name="layer",
    )(
        vert_count,
        slash_offsets,
        slash_count,
        vert_blocks,
        norm_gain.reshape(1, model),
        tokens,
        w_query,
        w_key,
        w_value,
        w_out,
        kv,
    )


def solution(mesh):
    return jax.shard_map(
        functools.partial(local, mesh.shape["seq"], mesh.shape["heads"] // 2),
        mesh=mesh,
        in_specs=(
            P("seq", None),
            P(),
            P(None, "heads"),
            P(None, "heads"),
            P(None, "heads"),
            P("heads", None),
            P("heads", "seq", None),
            P("heads", "seq", None),
            P("heads", None),
            P("heads"),
            P("heads", None),
            P("heads"),
        ),
        out_specs=P("seq", "heads"),
        check_vma=False,
    )
```

```python
import functools
import math

import jax
import jax.numpy as jnp
from jax import lax
from jax.experimental import pallas as pl
from jax.experimental.pallas import tpu as pltpu
from jax.sharding import PartitionSpec as P

BLK = 64
VCAP = 8
SMAX = 4
MESH = pl.DeviceIdType.MESH


def pick_kernel(vb, vc, ck, cv, kv, table, sems):
    heads, per_device = ck.shape[0], ck.shape[1] // BLK
    first = lax.axis_index("seq") * per_device
    stride = 2 * VCAP

    def copies(g, r, row):
        return [
            pltpu.make_async_copy(
                src.at[g, pl.ds(row, BLK)], kv.at[g, j, pl.ds(r * BLK, BLK)], sems.at[g, j, r]
            )
            for j, src in enumerate((ck, cv))
        ]

    for g in range(heads):
        count = jnp.int32(0)
        live = vc[g]
        for e in range(vb.shape[1]):
            block = vb[g, e] - first
            table[g * stride + count] = block
            mine = (e < live) & (block >= 0) & (block < per_device)
            count = count + mine.astype(jnp.int32)
        spare = jnp.where(count > 0, table[g * stride], 0)
        for r in range(VCAP):
            block = jnp.where(r < count, table[g * stride + r], spare)
            for copy in copies(g, r, pl.multiple_of(block * BLK, BLK)):
                copy.start()
    for g in range(heads):
        for r in range(VCAP):
            for copy in copies(g, r, 0):
                copy.wait()


def layer_kernel(
    n,
    chips,
    per_device,
    vc,
    so,
    sc,
    vb,
    gain,
    tok_hbm,
    wq_hbm,
    wk_hbm,
    wv_hbm,
    wo_hbm,
    kv_hbm,
    out,
    tok,
    normed,
    wq,
    wk,
    wv,
    wo,
    kv,
    near,
    prev,
    q,
    acc,
    mx,
    owner,
    att,
    core_out,
    core_in,
    x_out,
    x_in,
    part,
    load_sem,
    own_sem,
    send_sem,
    recv_sem,
    near_send,
    near_recv,
    core_send,
    core_recv,
    x_send,
    x_recv,
):
    head = lax.axis_index("heads")
    seq = lax.axis_index("seq")
    col, row = lax.rem(seq, 2), lax.div(seq, 2)
    other = 1 - col
    length = n // 2
    groups = kv.shape[1]
    hd, rows = q.shape[2], acc.shape[2]
    qheads = acc.shape[0]
    per = qheads // groups
    mate = row + 1 - 2 * lax.rem(row, 2)
    up = mate > row
    core_peer = head + 1 - 2 * lax.rem(head, 2)
    span_heads = 2 * chips

    def chip_peer(h, step):
        return lax.rem(h + 2 * step, span_heads)

    tile = wq.shape[1] // 4

    loads = [
        pltpu.make_async_copy(tok_hbm, tok, load_sem.at[0]),
        pltpu.make_async_copy(wk_hbm, wk, load_sem.at[1]),
        pltpu.make_async_copy(wv_hbm, wv, load_sem.at[2]),
    ]
    for j in range(4):
        cols = pl.ds(j * tile, tile)
        loads.append(pltpu.make_async_copy(wq_hbm.at[:, cols], wq.at[:, cols], load_sem.at[3 + j]))
    loads.append(pltpu.make_async_copy(wo_hbm, wo, load_sem.at[7]))
    own = pltpu.make_async_copy(kv_hbm, kv.at[seq], own_sem)
    own.start()
    for copy in loads[:4]:
        copy.start()

    barrier = pltpu.get_barrier_semaphore()

    def greet(h, s):
        pl.semaphore_signal(barrier, inc=1, device_id=(h, s), device_id_type=MESH)

    greet(core_peer, seq)
    for step in range(1, chips):
        greet(chip_peer(head, step), seq)
    greet(head, row * 2 + other)

    @pl.when(row > 0)
    def _():
        greet(head, seq - 2)

    @pl.when(row < length - 1)
    def _():
        greet(head, seq + 2)

    @pl.when(seq > 0)
    def _():
        greet(head, seq - 1)

    @pl.when(seq < n - 1)
    def _():
        greet(head, seq + 1)

    def flag(c):
        return jnp.where(c, 1, 0)

    pl.semaphore_wait(
        barrier,
        chips + 1 + flag(row > 0) + flag(row < length - 1) + flag(seq > 0) + flag(seq < n - 1),
    )

    def hop(s, g, way, src=None):
        target = (seq + 2, seq - 2, row * 2 + other)[way]
        return pltpu.make_async_remote_copy(
            src_ref=kv.at[s, g] if src is None else src.at[g],
            dst_ref=kv.at[s, g],
            send_sem=send_sem.at[way, s, g],
            recv_sem=recv_sem.at[s, g],
            device_id=(head, target),
            device_id_type=MESH,
        )

    for g in range(groups):

        @pl.when(row < length - 1)
        def _():
            hop(seq, g, 0, kv_hbm).start()

        @pl.when(row > 0)
        def _():
            hop(seq, g, 1, kv_hbm).start()

        hop(seq, g, 2, kv_hbm).start()

    loads[0].wait()
    for copy in loads[4:]:
        copy.start()

    @pl.loop(0, rows // 32)
    def _(i):
        span = pl.ds(pl.multiple_of(i * 32, 32), 32)
        a = tok[span, :].astype(jnp.float32)
        scale = lax.rsqrt(jnp.mean(a * a, axis=-1, keepdims=True) + 1e-05)
        normed[span, :] = (a * scale * gain[...]).astype(jnp.bfloat16)

    for j, w in enumerate((wk, wv)):
        loads[1 + j].wait()
        res = jnp.dot(normed[...], w[...], preferred_element_type=jnp.float32).astype(jnp.bfloat16)
        for g in range(groups):
            near[g, j] = res[:, g * hd : (g + 1) * hd]

    for j in range(4):
        loads[3 + j].wait()
        res = jnp.dot(
            normed[...], wq[:, j * tile : (j + 1) * tile], preferred_element_type=jnp.float32
        ).astype(jnp.bfloat16)
        for k in range(tile // hd):
            q[j * (tile // hd) + k] = res[:, k * hd : (k + 1) * hd]
        if j == 0:
            shift = pltpu.make_async_remote_copy(
                src_ref=near,
                dst_ref=prev,
                send_sem=near_send,
                recv_sem=near_recv,
                device_id=(head, jnp.where(seq < n - 1, seq + 1, seq - 1)),
                device_id_type=MESH,
            )

            @pl.when(seq < n - 1)
            def _():
                shift.start()

    def reach(t, d):
        r = row + t * (2 * d - 1)
        return r, (r >= 0) & (r < length)

    def across(r, g):
        return (r != mate) | (g < groups - 1)

    def relay(t):
        for g in range(groups):
            for d in range(2):
                r, ok = reach(t, d)

                @pl.when(ok)
                def _():
                    s = r * 2 + col
                    hop(s, g, 2).wait_recv()

                    @pl.when((row > 0) if d else (row < length - 1))
                    def _():
                        hop(s, g, 1 if d else 0).start()

                    @pl.when(across(r, g))
                    def _():
                        hop(s, g, 2).start()

    relay(1)

    factor = math.log2(math.e) / math.sqrt(hd)

    extra = acc.shape[1] - hd

    def fold(g, keys, values, allowed=None, live=None, some=None):
        heads = [g * per + k for k in range(per)]
        old = [(mx[h], acc[h]) for h in heads]
        fresh = []
        ones = jnp.ones((extra, keys.shape[0]), jnp.bfloat16)
        lhs = jnp.concatenate([jnp.transpose(values), ones], axis=0)
        if live is not None:
            lhs = lhs * live

        def score(h):
            res = lax.dot_general(
                keys, q[h], (((1,), (1,)), ((), ())), preferred_element_type=jnp.float32
            )
            return res if allowed is None else jnp.where(allowed, res, -jnp.inf)

        ahead = score(heads[0])
        for k, (m, a) in enumerate(old):
            scores = ahead
            if k + 1 < per:
                ahead = score(heads[k + 1])
            new = jnp.maximum(m, jnp.max(scores, axis=0, keepdims=True))
            weights = jnp.exp2((scores - new) * factor).astype(jnp.bfloat16)
            if some is not None:
                new = jnp.where(some, new, m)
            decay = jnp.exp2((m - new) * factor)
            a = a * decay + jnp.dot(lhs, weights, preferred_element_type=jnp.float32)
            fresh.append((new, a))
        for h, (m, a) in zip(heads, fresh):
            mx[h], acc[h] = m, a

    shape = (rows, rows)
    u_index = lax.broadcasted_iota(jnp.int32, shape, 0)
    t_index = lax.broadcasted_iota(jnp.int32, shape, 1)
    gap = t_index // BLK - u_index // BLK
    mx[...] = jnp.full(mx.shape, -1e30, jnp.float32)
    acc[...] = jnp.zeros(acc.shape, jnp.float32)

    def spans(g, rows_ref, offset):
        allowed = (gap + offset == 0) & (u_index <= t_index)
        for e in range(so.shape[1]):
            step = jnp.where(e < sc[g], so[g, e], -1)
            allowed = allowed | ((gap + offset == step) & (step >= 0))
        fold(g, rows_ref[g, 0], rows_ref[g, 1], allowed)
        return 0

    lax.fori_loop(0, groups, lambda g, _: spans(g, near, 0), 0)

    slots = kv.shape[3]
    slot_block = lax.broadcasted_iota(jnp.int32, (extra, slots), 1) // BLK
    slot_block = slot_block.astype(jnp.float32)
    entry = lax.broadcasted_iota(jnp.int32, (1, vb.shape[1]), 1)
    for g in range(groups):
        block = vb[g : g + 1, :]
        owner[g] = jnp.where((entry < vc[g]) & (block >= 0), lax.div(block, per_device), -1)

    def attend(s, g):
        held = jnp.where(owner[g] == s, 1.0, 0.0)
        count = jnp.sum(held, axis=1, keepdims=True)
        live = jnp.where(slot_block < count, 1.0, 0.0).astype(jnp.bfloat16)
        live = jnp.concatenate([live] * (acc.shape[1] // extra), axis=0)
        fold(g, kv[s, g, 0], kv[s, g, 1], live=live, some=count > 0)

    own.wait()

    def own_shard(g, _):
        attend(seq, g)
        return 0

    lax.fori_loop(0, groups, own_shard, 0)

    def visit(t, side, wait):
        def one(i, _):
            g, d = lax.div(i, 2), lax.rem(i, 2)
            r, ok = reach(t, d)
            if wait:
                ok = ok & ((t > 0) | (d == 0)) & across(r, g)

            @pl.when(ok)
            def _():
                s = r * 2 + side
                if wait:
                    hop(s, g, 2).wait_recv()
                attend(s, g)

            return 0

        lax.fori_loop(0, 2 * groups, one, 0)

    def rounds(t, _):
        visit(t, col, False)

        @pl.when(t < length - 1)
        def _():
            relay(t + 1)

        visit(t - 1, other, True)

        @pl.when((t == 1) & (seq > 0))
        def _():
            shift.wait_recv()
            lax.fori_loop(0, groups, lambda g, _: spans(g, prev, rows // BLK), 0)

        @pl.when((t == max(length - 2, 1)) & up)
        def _():
            hop(row * 2 + other, groups - 1, 0).start()

        @pl.when((t == max(length - 2, 1)) & jnp.logical_not(up))
        def _():
            hop(row * 2 + other, groups - 1, 1).start()

        return 0

    lax.fori_loop(1, length + 1, rounds, 0)
    last = mate * 2 + other
    hop(last, groups - 1, 2).wait_recv()
    attend(last, groups - 1)

    for h in range(qheads):
        att[:, h * hd : (h + 1) * hd] = jnp.transpose(acc[h, :hd] / acc[h, hd : hd + 1]).astype(jnp.bfloat16)

    loads[7].wait()
    width = part.shape[2]
    pieces = out.shape[1] // width

    def product(target, j):
        start = pl.multiple_of(target * out.shape[1] + j * width, width)
        return jnp.dot(att[...], wo[:, pl.ds(start, width)], preferred_element_type=jnp.float32)

    def core_copy(i):
        return pltpu.make_async_remote_copy(
            src_ref=core_out.at[i],
            dst_ref=core_in.at[i],
            send_sem=core_send.at[i],
            recv_sem=core_recv.at[i],
            device_id=(core_peer, seq),
            device_id_type=MESH,
        )

    def x_copy(step, j):
        i = (step - 1) * pieces + j
        return pltpu.make_async_remote_copy(
            src_ref=x_out.at[i],
            dst_ref=x_in.at[i],
            send_sem=x_send.at[i],
            recv_sem=x_recv.at[i],
            device_id=(chip_peer(head, step), seq),
            device_id_type=MESH,
        )

    todo = [(step, j) for step in range(1, chips + 1) for j in range(pieces)]

    def exchange(i):
        step, j = todo[i]
        core_out[i] = product(chip_peer(core_peer, step), j).astype(jnp.bfloat16)
        core_copy(i).start()
        part[i] = product(chip_peer(head, step), j)

    def combine(i):
        step, j = todo[i]
        core_copy(i).wait_recv()
        both = part[i] + core_in[i].astype(jnp.float32)
        if step < chips:
            x_out[i] = both.astype(jnp.bfloat16)
        else:
            part[i] = both

    def forward(i):
        combine(i)
        if todo[i][0] < chips:
            x_copy(*todo[i]).start()

    lag = min(2, len(todo))
    for i in range(len(todo)):
        exchange(i)
        if i >= lag:
            forward(i - lag)
    for i in range(len(todo) - lag, len(todo)):
        forward(i)
    for j in range(pieces):
        total = part[len(todo) - pieces + j]
        for step in range(1, chips):
            x_copy(step, j).wait_recv()
            total = total + x_in[(step - 1) * pieces + j].astype(jnp.float32)
        out[:, j * width : (j + 1) * width] = total.astype(jnp.bfloat16)
    for i, (step, j) in enumerate(todo):
        core_copy(i).wait_send()
        if step < chips:
            x_copy(step, j).wait_send()

    @pl.when(seq < n - 1)
    def _():
        shift.wait_send()

    def settle(t, _):
        for g in range(groups):
            for d in range(2):
                r, ok = reach(t, d)
                once = ok if d else ok & (t > 0)

                @pl.when(once)
                def _():
                    s = r * 2 + col

                    @pl.when(across(r, g))
                    def _():
                        hop(s, g, 2).wait_send()

                    @pl.when((row > 0) & ((t == 0) | (d == 1)))
                    def _():
                        hop(s, g, 1).wait_send()

                    @pl.when((row < length - 1) & ((t == 0) | (d == 0)))
                    def _():
                        hop(s, g, 0).wait_send()

        return 0

    lax.fori_loop(0, length, settle, 0)

    @pl.when(up)
    def _():
        hop(row * 2 + other, groups - 1, 0).wait_send()

    @pl.when(jnp.logical_not(up))
    def _():
        hop(row * 2 + other, groups - 1, 1).wait_send()


def local(
    n,
    chips,
    tokens,
    norm_gain,
    w_query,
    w_key,
    w_value,
    w_out,
    cache_keys,
    cache_values,
    vert_blocks,
    vert_count,
    slash_offsets,
    slash_count,
):
    groups, _, hd = cache_keys.shape
    rows, model = tokens.shape
    qcols = w_query.shape[1]
    qheads = qcols // hd
    out_cols = w_out.shape[1] // (2 * chips)
    slots = VCAP * BLK
    bf16, f32 = jnp.bfloat16, jnp.float32
    smem = pl.BlockSpec(memory_space=pltpu.SMEM)
    vmem = pl.BlockSpec(memory_space=pltpu.VMEM)
    hbm = pl.BlockSpec(memory_space=pl.ANY)
    kv = pl.pallas_call(
        pick_kernel,
        out_shape=jax.ShapeDtypeStruct((groups, 2, slots, hd), bf16),
        in_specs=[smem] * 2 + [hbm] * 2,
        out_specs=vmem,
        scratch_shapes=[
            pltpu.SMEM((groups * 2 * VCAP,), jnp.int32),
            pltpu.SemaphoreType.DMA((groups, 2, VCAP)),
        ],
        compiler_params=pltpu.CompilerParams(vmem_limit_bytes=60 << 20),
        name="pick",
    )(vert_blocks, vert_count, cache_keys, cache_values)
    pieces = 4
    width = out_cols // pieces
    dma = pltpu.SemaphoreType.DMA
    return pl.pallas_call(
        functools.partial(layer_kernel, n, chips, cache_keys.shape[1] // BLK),
        out_shape=jax.ShapeDtypeStruct((rows, out_cols), bf16),
        in_specs=[smem] * 3 + [vmem] * 2 + [hbm] * 6,
        out_specs=vmem,
        scratch_shapes=[
            pltpu.VMEM((rows, model), bf16),
            pltpu.VMEM((rows, model), bf16),
            pltpu.VMEM(w_query.shape, bf16),
            pltpu.VMEM(w_key.shape, bf16),
            pltpu.VMEM(w_value.shape, bf16),
            pltpu.VMEM(w_out.shape, bf16),
            pltpu.VMEM((n, groups, 2, slots, hd), bf16),
            pltpu.VMEM((groups, 2, rows, hd), bf16),
            pltpu.VMEM((groups, 2, rows, hd), bf16),
            pltpu.VMEM((qheads, rows, hd), bf16),
            pltpu.VMEM((qheads, hd + 16, rows), f32),
            pltpu.VMEM((qheads, 1, rows), f32),
            pltpu.VMEM((groups, 1, vert_blocks.shape[1]), jnp.int32),
            pltpu.VMEM((rows, qcols), bf16),
            pltpu.VMEM((chips * pieces, rows, width), bf16),
            pltpu.VMEM((chips * pieces, rows, width), bf16),
            pltpu.VMEM(((chips - 1) * pieces, rows, width), bf16),
            pltpu.VMEM(((chips - 1) * pieces, rows, width), bf16),
            pltpu.VMEM((chips * pieces, rows, width), f32),
            dma((8,)),
            dma(()),
            dma((3, n, groups)),
            dma((n, groups)),
            dma(()),
            dma(()),
            dma((chips * pieces,)),
            dma((chips * pieces,)),
            dma(((chips - 1) * pieces,)),
            dma(((chips - 1) * pieces,)),
        ],
        compiler_params=pltpu.CompilerParams(
            collective_id=0, has_side_effects=True, vmem_limit_bytes=60 << 20
        ),
        name="layer",
    )(
        vert_count,
        slash_offsets,
        slash_count,
        vert_blocks,
        norm_gain.reshape(1, model),
        tokens,
        w_query,
        w_key,
        w_value,
        w_out,
        kv,
    )


def solution(mesh):
    return jax.shard_map(
        functools.partial(local, mesh.shape["seq"], mesh.shape["heads"] // 2),
        mesh=mesh,
        in_specs=(
            P("seq", None),
            P(),
            P(None, "heads"),
            P(None, "heads"),
            P(None, "heads"),
            P("heads", None),
            P("heads", "seq", None),
            P("heads", "seq", None),
            P("heads", None),
            P("heads"),
            P("heads", None),
            P("heads"),
        ),
        out_specs=P("seq", "heads"),
        check_vma=False,
    )
```

```python
import functools
import math

import jax
import jax.numpy as jnp
from jax import lax
from jax.experimental import pallas as pl
from jax.experimental.pallas import tpu as pltpu
from jax.sharding import PartitionSpec as P

BLK = 64
VCAP = 8
SMAX = 4
MESH = pl.DeviceIdType.MESH


def pick_kernel(vb, vc, ck, cv, kv, table, sems):
    heads, per_device = ck.shape[0], ck.shape[1] // BLK
    first = lax.axis_index("seq") * per_device
    stride = 2 * VCAP

    def copies(g, r, row):
        return [
            pltpu.make_async_copy(
                src.at[g, pl.ds(row, BLK)], kv.at[g, j, pl.ds(r * BLK, BLK)], sems.at[g, j, r]
            )
            for j, src in enumerate((ck, cv))
        ]

    for g in range(heads):
        count = jnp.int32(0)
        live = vc[g]
        for e in range(vb.shape[1]):
            block = vb[g, e] - first
            table[g * stride + count] = block
            mine = (e < live) & (block >= 0) & (block < per_device)
            count = count + mine.astype(jnp.int32)
        spare = jnp.where(count > 0, table[g * stride], 0)
        for r in range(VCAP):
            block = jnp.where(r < count, table[g * stride + r], spare)
            for copy in copies(g, r, pl.multiple_of(block * BLK, BLK)):
                copy.start()
    for g in range(heads):
        for r in range(VCAP):
            for copy in copies(g, r, 0):
                copy.wait()


def layer_kernel(
    n,
    chips,
    per_device,
    vc,
    so,
    sc,
    vb,
    gain,
    tok_hbm,
    wq_hbm,
    wk_hbm,
    wv_hbm,
    wo_hbm,
    kv_hbm,
    out,
    tok,
    normed,
    wq,
    wk,
    wv,
    wo,
    kv,
    near,
    prev,
    near2,
    prev2,
    q,
    q2,
    acc,
    mx,
    owner,
    att,
    attb,
    core_out,
    core_in,
    x_out,
    x_in,
    part,
    load_sem,
    own_sem,
    send_sem,
    recv_sem,
    near_send,
    near_recv,
    side_send,
    side_recv,
    core_send,
    core_recv,
    x_send,
    x_recv,
):
    head = lax.axis_index("heads")
    seq = lax.axis_index("seq")
    col, row = lax.rem(seq, 2), lax.div(seq, 2)
    other = 1 - col
    length = n // 2
    groups = kv.shape[1]
    hd, rows = q.shape[2], acc.shape[2]
    qheads = q.shape[0]
    per = qheads // groups
    pair = groups == 2 and length % 2 == 0
    mine = lax.rem(row, 2) if pair else 0
    theirs = 1 - mine if pair else 0
    mate = seq + 2 - 4 * mine

    def up_ok(g):
        return row < length - (2 if pair and g == 0 else 1)

    def down_ok(g):
        return row > (1 if pair and g == 1 else 0)

    def get_ok(g, d):
        if d:
            return row >= (1 if pair and g == 1 else 0)
        return row < length - (1 if pair and g == 0 else 0)
    core_peer = head + 1 - 2 * lax.rem(head, 2)
    span_heads = 2 * chips

    def chip_peer(h, step):
        return lax.rem(h + 2 * step, span_heads)

    tile = wq.shape[1] // 4

    def columns(j):
        return pl.ds(pl.multiple_of(lax.rem(j + 2 * theirs, 4) * tile, tile), tile)

    def sided(i, src, dst):
        return pltpu.make_async_remote_copy(
            src_ref=src,
            dst_ref=dst,
            send_sem=side_send.at[i],
            recv_sem=side_recv.at[i],
            device_id=(head, mate),
            device_id_type=MESH,
        )

    lend_q = sided(0, q.at[pl.ds(theirs * per, per)], q2)
    lend_near = sided(1, near.at[theirs], near2)
    lend_prev = sided(2, prev.at[theirs], prev2)

    def give(p):
        return sided(3 + p, attb.at[p], att.at[mine * 2 + p])

    loads = [
        pltpu.make_async_copy(tok_hbm, tok, load_sem.at[0]),
        pltpu.make_async_copy(wk_hbm, wk, load_sem.at[1]),
        pltpu.make_async_copy(wv_hbm, wv, load_sem.at[2]),
    ]
    for j in range(4):
        cols = columns(j)
        loads.append(pltpu.make_async_copy(wq_hbm.at[:, cols], wq.at[:, cols], load_sem.at[3 + j]))
    loads.append(pltpu.make_async_copy(wo_hbm, wo, load_sem.at[7]))
    own = pltpu.make_async_copy(kv_hbm, kv.at[seq], own_sem)
    own.start()
    for copy in loads[:4]:
        copy.start()

    barrier = pltpu.get_barrier_semaphore()

    def greet(h, s):
        pl.semaphore_signal(barrier, inc=1, device_id=(h, s), device_id_type=MESH)

    greet(core_peer, seq)
    for step in range(1, chips):
        greet(chip_peer(head, step), seq)
    greet(head, row * 2 + other)

    @pl.when(row > 0)
    def _():
        greet(head, seq - 2)

    @pl.when(row < length - 1)
    def _():
        greet(head, seq + 2)

    @pl.when(seq > 0)
    def _():
        greet(head, seq - 1)

    @pl.when(seq < n - 1)
    def _():
        greet(head, seq + 1)

    def flag(c):
        return jnp.where(c, 1, 0)

    pl.semaphore_wait(
        barrier,
        chips + 1 + flag(row > 0) + flag(row < length - 1) + flag(seq > 0) + flag(seq < n - 1),
    )

    def hop(s, g, way, src=None):
        target = (seq + 2, seq - 2, row * 2 + other)[way]
        return pltpu.make_async_remote_copy(
            src_ref=kv.at[s, g] if src is None else src.at[g],
            dst_ref=kv.at[s, g],
            send_sem=send_sem.at[way, s, g],
            recv_sem=recv_sem.at[s, g],
            device_id=(head, target),
            device_id_type=MESH,
        )

    ahead = [(groups - 1, 0), (0, 1)]
    behind = [(0, 0), (1, 1)] if groups > 1 else []
    for i, (g, d) in enumerate(ahead + behind):

        @pl.when(down_ok(g) if d else up_ok(g))
        def _():
            hop(seq, g, d, kv_hbm).start()

        if i == 1:
            hop(seq, mine, 2, kv_hbm).start()

    loads[0].wait()
    for copy in loads[4:]:
        copy.start()

    @pl.loop(0, rows // 32)
    def _(i):
        span = pl.ds(pl.multiple_of(i * 32, 32), 32)
        a = tok[span, :].astype(jnp.float32)
        scale = lax.rsqrt(jnp.mean(a * a, axis=-1, keepdims=True) + 1e-05)
        normed[span, :] = (a * scale * gain[...]).astype(jnp.bfloat16)

    for j, w in enumerate((wk, wv)):
        loads[1 + j].wait()
        res = jnp.dot(normed[...], w[...], preferred_element_type=jnp.float32).astype(jnp.bfloat16)
        for g in range(groups):
            near[g, j] = res[:, g * hd : (g + 1) * hd]

    shift = pltpu.make_async_remote_copy(
        src_ref=near,
        dst_ref=prev,
        send_sem=near_send,
        recv_sem=near_recv,
        device_id=(head, jnp.where(seq < n - 1, seq + 1, seq - 1)),
        device_id_type=MESH,
    )

    @pl.when(seq < n - 1)
    def _():
        shift.start()

    if pair:
        lend_near.start()

    for j in range(4):
        loads[3 + j].wait()
        res = jnp.dot(
            normed[...], wq[:, columns(j)], preferred_element_type=jnp.float32
        ).astype(jnp.bfloat16)
        for k in range(tile // hd):
            q[lax.rem(j + 2 * theirs, 4) * (tile // hd) + k] = res[:, k * hd : (k + 1) * hd]
        if pair and j == 1:
            lend_q.start()

    def reach(t, d):
        r = row + t * (2 * d - 1)
        return r, (r >= 0) & (r < length)

    def relay(t, which):
        for g, d in which:
            r, ok = reach(t, d)

            @pl.when(ok & get_ok(g, d))
            def _():
                s = r * 2 + col
                hop(s, g, 2).wait_recv()

                @pl.when(down_ok(g) if d else up_ok(g))
                def _():
                    hop(s, g, d).start()

                @pl.when(g == mine)
                def _():
                    hop(s, g, 2).start()

    relay(1, ahead)

    factor = math.log2(math.e) / math.sqrt(hd)

    extra = acc.shape[1] - hd

    def fold(sets, keys, values, allowed=None, live=None, some=None):
        heads = [i * per + k for i in sets for k in range(per)]
        old = [(mx[h], acc[h]) for h in heads]
        fresh = []
        ones = jnp.ones((extra, keys.shape[0]), jnp.bfloat16)
        lhs = jnp.concatenate([jnp.transpose(values), ones], axis=0)
        if live is not None:
            lhs = lhs * live

        def score(h):
            queries = q[mine * per + h] if h < per else q2[h - per]
            res = lax.dot_general(
                keys, queries, (((1,), (1,)), ((), ())), preferred_element_type=jnp.float32
            )
            return res if allowed is None else jnp.where(allowed, res, -jnp.inf)

        ahead = score(heads[0])
        for k, (m, a) in enumerate(old):
            scores = ahead
            if k + 1 < len(heads):
                ahead = score(heads[k + 1])
            new = jnp.maximum(m, jnp.max(scores, axis=0, keepdims=True))
            weights = jnp.exp2((scores - new) * factor).astype(jnp.bfloat16)
            if some is not None:
                new = jnp.where(some, new, m)
            decay = jnp.exp2((m - new) * factor)
            a = a * decay + jnp.dot(lhs, weights, preferred_element_type=jnp.float32)
            fresh.append((new, a))
        for h, (m, a) in zip(heads, fresh):
            mx[h], acc[h] = m, a

    shape = (rows, rows)
    u_index = lax.broadcasted_iota(jnp.int32, shape, 0)
    t_index = lax.broadcasted_iota(jnp.int32, shape, 1)
    gap = t_index // BLK - u_index // BLK
    mx[...] = jnp.full(mx.shape, -1e30, jnp.float32)
    acc[...] = jnp.zeros(acc.shape, jnp.float32)

    def spans(i, span, offset):
        allowed = (gap + offset == 0) & (u_index <= t_index)
        for e in range(so.shape[1]):
            step = jnp.where(e < sc[mine], so[mine, e], -1)
            allowed = allowed | ((gap + offset == step) & (step >= 0))
        fold([i], span[0], span[1], allowed)

    spans(0, near.at[mine], 0)
    relay(1, behind)

    slots = kv.shape[3]
    slot_block = lax.broadcasted_iota(jnp.int32, (extra, slots), 1) // BLK
    slot_block = slot_block.astype(jnp.float32)
    entry = lax.broadcasted_iota(jnp.int32, (1, vb.shape[1]), 1)
    for g in range(groups):
        block = vb[g : g + 1, :]
        owner[g] = jnp.where((entry < vc[g]) & (block >= 0), lax.div(block, per_device), -1)

    sets = [0, 1] if pair else [0]

    both = [0, 1] if pair else [0]

    def attend(s, sets):
        held = jnp.where(owner[mine] == s, 1.0, 0.0)
        count = jnp.sum(held, axis=1, keepdims=True)
        live = jnp.where(slot_block < count, 1.0, 0.0).astype(jnp.bfloat16)
        live = jnp.concatenate([live] * (acc.shape[1] // extra), axis=0)
        fold(sets, kv[s, mine, 0], kv[s, mine, 1], live=live, some=count > 0)

    def visit(t, side, wait, sets):
        def one(d, _):
            r, ok = reach(t, d)
            if side is other:
                ok = ok & ((t > 0) | (d == 0))

            @pl.when(ok)
            def _():
                s = r * 2 + side
                if wait:
                    hop(s, mine, 2).wait_recv()
                attend(s, sets)

            return 0

        lax.fori_loop(0, 2, one, 0)

    def first(sets):
        def one(i, _):
            r = row + i - 1

            @pl.when((r >= 0) & (r < length))
            def _():
                attend(r * 2 + col, sets)

            return 0

        lax.fori_loop(0, 3, one, 0)

    own.wait()
    first([0])

    @pl.when(seq > 0)
    def _():
        shift.wait_recv()
        if pair:
            lend_prev.start()

    def rounds(t, _):
        @pl.when(t > 1)
        def _():
            visit(t, col, False, both)

        @pl.when(t < length - 1)
        def _():
            relay(t + 1, ahead)

        @pl.when((t == 1) & (seq > 0))
        def _():
            spans(0, prev.at[mine], rows // BLK)

        if pair:

            @pl.when(t == 1)
            def _():
                lend_q.wait_recv()
                first([1])
                lend_near.wait_recv()
                spans(1, near2, 0)

        @pl.when(t < length - 1)
        def _():
            relay(t + 1, behind)

        visit(t - 1, other, True, both)

        if pair:

            @pl.when((t == 1) & (mate > 0))
            def _():
                lend_prev.wait_recv()
                spans(1, prev2, rows // BLK)

        return 0

    lax.fori_loop(1, length, rounds, 0)
    visit(length - 1, other, True, both[-1:])

    half = att.shape[2] // hd

    def settled(h):
        return jnp.transpose(acc[h, :hd] / acc[h, hd : hd + 1]).astype(jnp.bfloat16)

    if pair:
        for p in range(2):
            for k in range(half):
                attb[p, :, k * hd : (k + 1) * hd] = settled(per + p * half + k)
            give(p).start()
        visit(length - 1, other, False, [0])
    for p in range(2):
        for k in range(half):
            att[mine * 2 + p, :, k * hd : (k + 1) * hd] = settled(p * half + k)
    if pair:
        for p in range(2):
            sided(3 + p, attb.at[p], att.at[theirs * 2 + p]).wait_recv()

    loads[7].wait()
    width = part.shape[2]
    pieces = out.shape[1] // width

    def product(target, j):
        start = pl.multiple_of(target * out.shape[1] + j * width, width)
        total = None
        for p in range(att.shape[0]):
            rows_of = slice(p * att.shape[2], (p + 1) * att.shape[2])
            res = jnp.dot(
                att[p], wo[rows_of, pl.ds(start, width)], preferred_element_type=jnp.float32
            )
            total = res if total is None else total + res
        return total

    def core_copy(i):
        return pltpu.make_async_remote_copy(
            src_ref=core_out.at[i],
            dst_ref=core_in.at[i],
            send_sem=core_send.at[i],
            recv_sem=core_recv.at[i],
            device_id=(core_peer, seq),
            device_id_type=MESH,
        )

    def x_copy(step, j):
        i = (step - 1) * pieces + j
        return pltpu.make_async_remote_copy(
            src_ref=x_out.at[i],
            dst_ref=x_in.at[i],
            send_sem=x_send.at[i],
            recv_sem=x_recv.at[i],
            device_id=(chip_peer(head, step), seq),
            device_id_type=MESH,
        )

    todo = [(step, j) for step in range(1, chips + 1) for j in range(pieces)]

    def exchange(i):
        step, j = todo[i]
        core_out[i] = product(chip_peer(core_peer, step), j).astype(jnp.bfloat16)
        core_copy(i).start()
        part[i] = product(chip_peer(head, step), j)

    def combine(i):
        step, j = todo[i]
        core_copy(i).wait_recv()
        both = part[i] + core_in[i].astype(jnp.float32)
        if step < chips:
            x_out[i] = both.astype(jnp.bfloat16)
        else:
            part[i] = both

    def forward(i):
        combine(i)
        if todo[i][0] < chips:
            x_copy(*todo[i]).start()

    lag = min(2, len(todo))
    for i in range(len(todo)):
        exchange(i)
        if i >= lag:
            forward(i - lag)
    for i in range(len(todo) - lag, len(todo)):
        forward(i)
    for j in range(pieces):
        total = part[len(todo) - pieces + j]
        for step in range(1, chips):
            x_copy(step, j).wait_recv()
            total = total + x_in[(step - 1) * pieces + j].astype(jnp.float32)
        out[:, j * width : (j + 1) * width] = total.astype(jnp.bfloat16)
    for i, (step, j) in enumerate(todo):
        core_copy(i).wait_send()
        if step < chips:
            x_copy(step, j).wait_send()

    @pl.when(seq < n - 1)
    def _():
        shift.wait_send()

    if pair:
        lend_q.wait_send()
        lend_near.wait_send()

        @pl.when(seq > 0)
        def _():
            lend_prev.wait_send()

        for p in range(2):
            give(p).wait_send()

    def settle(t, _):
        for g in range(groups):
            for d in range(2):
                r, ok = reach(t, d)
                once = (ok if d else ok & (t > 0)) & ((t == 0) | get_ok(g, d))

                @pl.when(once)
                def _():
                    s = r * 2 + col

                    @pl.when(g == mine)
                    def _():
                        hop(s, g, 2).wait_send()

                    @pl.when(down_ok(g) & ((t == 0) | (d == 1)))
                    def _():
                        hop(s, g, 1).wait_send()

                    @pl.when(up_ok(g) & ((t == 0) | (d == 0)))
                    def _():
                        hop(s, g, 0).wait_send()

        return 0

    lax.fori_loop(0, length, settle, 0)


def local(
    n,
    chips,
    tokens,
    norm_gain,
    w_query,
    w_key,
    w_value,
    w_out,
    cache_keys,
    cache_values,
    vert_blocks,
    vert_count,
    slash_offsets,
    slash_count,
):
    groups, _, hd = cache_keys.shape
    rows, model = tokens.shape
    qcols = w_query.shape[1]
    qheads = qcols // hd
    per = qheads // groups
    out_cols = w_out.shape[1] // (2 * chips)
    slots = VCAP * BLK
    bf16, f32 = jnp.bfloat16, jnp.float32
    smem = pl.BlockSpec(memory_space=pltpu.SMEM)
    vmem = pl.BlockSpec(memory_space=pltpu.VMEM)
    hbm = pl.BlockSpec(memory_space=pl.ANY)
    kv = pl.pallas_call(
        pick_kernel,
        out_shape=jax.ShapeDtypeStruct((groups, 2, slots, hd), bf16),
        in_specs=[smem] * 2 + [hbm] * 2,
        out_specs=vmem,
        scratch_shapes=[
            pltpu.SMEM((groups * 2 * VCAP,), jnp.int32),
            pltpu.SemaphoreType.DMA((groups, 2, VCAP)),
        ],
        compiler_params=pltpu.CompilerParams(vmem_limit_bytes=60 << 20),
        name="pick",
    )(vert_blocks, vert_count, cache_keys, cache_values)
    pieces = 4
    width = out_cols // pieces
    dma = pltpu.SemaphoreType.DMA
    return pl.pallas_call(
        functools.partial(layer_kernel, n, chips, cache_keys.shape[1] // BLK),
        out_shape=jax.ShapeDtypeStruct((rows, out_cols), bf16),
        in_specs=[smem] * 3 + [vmem] * 2 + [hbm] * 6,
        out_specs=vmem,
        scratch_shapes=[
            pltpu.VMEM((rows, model), bf16),
            pltpu.VMEM((rows, model), bf16),
            pltpu.VMEM(w_query.shape, bf16),
            pltpu.VMEM(w_key.shape, bf16),
            pltpu.VMEM(w_value.shape, bf16),
            pltpu.VMEM(w_out.shape, bf16),
            pltpu.VMEM((n, groups, 2, slots, hd), bf16),
            pltpu.VMEM((groups, 2, rows, hd), bf16),
            pltpu.VMEM((groups, 2, rows, hd), bf16),
            pltpu.VMEM((2, rows, hd), bf16),
            pltpu.VMEM((2, rows, hd), bf16),
            pltpu.VMEM((qheads, rows, hd), bf16),
            pltpu.VMEM((per, rows, hd), bf16),
            pltpu.VMEM((2 * per, hd + 16, rows), f32),
            pltpu.VMEM((2 * per, 1, rows), f32),
            pltpu.VMEM((groups, 1, vert_blocks.shape[1]), jnp.int32),
            pltpu.VMEM((2 * groups, rows, qcols // (2 * groups)), bf16),
            pltpu.VMEM((2, rows, qcols // (2 * groups)), bf16),
            pltpu.VMEM((chips * pieces, rows, width), bf16),
            pltpu.VMEM((chips * pieces, rows, width), bf16),
            pltpu.VMEM(((chips - 1) * pieces, rows, width), bf16),
            pltpu.VMEM(((chips - 1) * pieces, rows, width), bf16),
            pltpu.VMEM((chips * pieces, rows, width), f32),
            dma((8,)),
            dma(()),
            dma((3, n, groups)),
            dma((n, groups)),
            dma(()),
            dma(()),
            dma((5,)),
            dma((5,)),
            dma((chips * pieces,)),
            dma((chips * pieces,)),
            dma(((chips - 1) * pieces,)),
            dma(((chips - 1) * pieces,)),
        ],
        compiler_params=pltpu.CompilerParams(
            collective_id=0, has_side_effects=True, vmem_limit_bytes=60 << 20
        ),
        name="layer",
    )(
        vert_count,
        slash_offsets,
        slash_count,
        vert_blocks,
        norm_gain.reshape(1, model),
        tokens,
        w_query,
        w_key,
        w_value,
        w_out,
        kv,
    )


def solution(mesh):
    return jax.shard_map(
        functools.partial(local, mesh.shape["seq"], mesh.shape["heads"] // 2),
        mesh=mesh,
        in_specs=(
            P("seq", None),
            P(),
            P(None, "heads"),
            P(None, "heads"),
            P(None, "heads"),
            P("heads", None),
            P("heads", "seq", None),
            P("heads", "seq", None),
            P("heads", None),
            P("heads"),
            P("heads", None),
            P("heads"),
        ),
        out_specs=P("seq", "heads"),
        check_vma=False,
    )
```

```python
import functools
import math

import jax
import jax.numpy as jnp
from jax import lax
from jax.experimental import pallas as pl
from jax.experimental.pallas import tpu as pltpu
from jax.sharding import PartitionSpec as P

BLK = 64
VCAP = 8
SMAX = 4
MESH = pl.DeviceIdType.MESH


def pick_kernel(vb, vc, ck, cv, kv, table, sems):
    heads, per_device = ck.shape[0], ck.shape[1] // BLK
    first = lax.axis_index("seq") * per_device
    stride = 2 * VCAP

    def copies(g, r, row):
        return [
            pltpu.make_async_copy(
                src.at[g, pl.ds(row, BLK)], kv.at[g, j, pl.ds(r * BLK, BLK)], sems.at[g, j, r]
            )
            for j, src in enumerate((ck, cv))
        ]

    for g in range(heads):
        count = jnp.int32(0)
        live = vc[g]
        for e in range(vb.shape[1]):
            block = vb[g, e] - first
            table[g * stride + count] = block
            mine = (e < live) & (block >= 0) & (block < per_device)
            count = count + mine.astype(jnp.int32)
        spare = jnp.where(count > 0, table[g * stride], 0)
        for r in range(VCAP):
            block = jnp.where(r < count, table[g * stride + r], spare)
            for copy in copies(g, r, pl.multiple_of(block * BLK, BLK)):
                copy.start()
    for g in range(heads):
        for r in range(VCAP):
            for copy in copies(g, r, 0):
                copy.wait()


def layer_kernel(
    n,
    chips,
    per_device,
    vc,
    so,
    sc,
    vb,
    gain,
    tok_hbm,
    wq_hbm,
    wk_hbm,
    wv_hbm,
    wo_hbm,
    kv_hbm,
    out,
    tok,
    normed,
    wq,
    wk,
    wv,
    wo,
    kv,
    near,
    prev,
    near2,
    prev2,
    q,
    q2,
    acc,
    mx,
    owner,
    att,
    attb,
    core_out,
    core_in,
    x_out,
    x_in,
    part,
    load_sem,
    own_sem,
    send_sem,
    recv_sem,
    near_send,
    near_recv,
    side_send,
    side_recv,
    core_send,
    core_recv,
    x_send,
    x_recv,
):
    head = lax.axis_index("heads")
    seq = lax.axis_index("seq")
    col, row = lax.rem(seq, 2), lax.div(seq, 2)
    other = 1 - col
    length = n // 2
    groups = kv.shape[1]
    hd, rows = q.shape[2], acc.shape[2]
    qheads = q.shape[0]
    per = qheads // groups
    pair = groups == 2 and length % 2 == 0
    mine = lax.rem(row, 2) if pair else 0
    theirs = 1 - mine if pair else 0
    mate = seq + 2 - 4 * mine

    def up_ok(g):
        return row < length - (2 if pair and g == 0 else 1)

    def down_ok(g):
        return row > (1 if pair and g == 1 else 0)

    def get_ok(g, d):
        if d:
            return row >= (1 if pair and g == 1 else 0)
        return row < length - (1 if pair and g == 0 else 0)
    core_peer = head + 1 - 2 * lax.rem(head, 2)
    span_heads = 2 * chips

    def chip_peer(h, step):
        return lax.rem(h + 2 * step, span_heads)

    tile = wq.shape[1] // 4

    def columns(j):
        return pl.ds(pl.multiple_of(lax.rem(j + 2 * theirs, 4) * tile, tile), tile)

    def sided(i, src, dst):
        return pltpu.make_async_remote_copy(
            src_ref=src,
            dst_ref=dst,
            send_sem=side_send.at[i],
            recv_sem=side_recv.at[i],
            device_id=(head, mate),
            device_id_type=MESH,
        )

    lend_q = sided(0, q.at[pl.ds(theirs * per, per)], q2)
    lend_near = sided(1, near.at[theirs], near2)
    after = jnp.where(seq < n - 1, seq + 1, seq - 1)
    after_group = lax.rem(lax.div(after, 2), 2) if pair else 0
    shift = pltpu.make_async_remote_copy(
        src_ref=near.at[after_group],
        dst_ref=prev,
        send_sem=near_send,
        recv_sem=near_recv,
        device_id=(head, after),
        device_id_type=MESH,
    )
    crossing = (col == 1) & (mine == 1) & (row < length - 1)

    def before(src, own_rows, target, sem):
        return pltpu.make_async_remote_copy(
            src_ref=src,
            dst_ref=prev if own_rows else prev2,
            send_sem=side_send.at[sem],
            recv_sem=near_recv if own_rows else side_recv.at[2],
            device_id=(head, target),
            device_id_type=MESH,
        )

    def beside(src, own_rows):
        return before(src, own_rows, row * 2 + other, 5 if own_rows else 2)

    cross = [
        before(near.at[0], True, jnp.minimum(seq + 1, n - 1), 6),
        before(near.at[groups - 1], False, jnp.minimum(seq + 3, n - 1), 7),
    ]

    def give(p):
        part_rows = pl.ds(p * (rows // 2), rows // 2)
        return sided(3 + p, attb.at[part_rows], att.at[mine, part_rows])

    loads = [
        pltpu.make_async_copy(tok_hbm, tok, load_sem.at[0]),
        pltpu.make_async_copy(wk_hbm, wk, load_sem.at[1]),
        pltpu.make_async_copy(wv_hbm, wv, load_sem.at[2]),
    ]
    for j in range(4):
        cols = columns(j)
        loads.append(pltpu.make_async_copy(wq_hbm.at[:, cols], wq.at[:, cols], load_sem.at[3 + j]))
    loads.append(pltpu.make_async_copy(wo_hbm, wo, load_sem.at[7]))
    own = pltpu.make_async_copy(kv_hbm, kv.at[seq], own_sem)
    own.start()
    for copy in loads[:4]:
        copy.start()

    barrier = pltpu.get_barrier_semaphore()

    def greet(h, s):
        pl.semaphore_signal(barrier, inc=1, device_id=(h, s), device_id_type=MESH)

    greet(core_peer, seq)
    for step in range(1, chips):
        greet(chip_peer(head, step), seq)
    greet(head, row * 2 + other)

    @pl.when(row > 0)
    def _():
        greet(head, seq - 2)

    @pl.when(row < length - 1)
    def _():
        greet(head, seq + 2)

    if pair:
        crossed = (col == 0) & (row > 1)

        @pl.when(crossed)
        def _():
            greet(head, seq - 1 - 2 * mine)

    else:

        @pl.when(seq > 0)
        def _():
            greet(head, seq - 1)

    def flag(c):
        return jnp.where(c, 1, 0)

    pl.semaphore_wait(
        barrier,
        chips
        + 1
        + flag(row > 0)
        + flag(row < length - 1)
        + (2 * flag(crossing) if pair else flag(seq < n - 1)),
    )

    def hop(s, g, way, src=None):
        target = (seq + 2, seq - 2, row * 2 + other)[way]
        return pltpu.make_async_remote_copy(
            src_ref=kv.at[s, g] if src is None else src.at[g],
            dst_ref=kv.at[s, g],
            send_sem=send_sem.at[way, s, g],
            recv_sem=recv_sem.at[s, g],
            device_id=(head, target),
            device_id_type=MESH,
        )

    ahead = [(groups - 1, 0), (0, 1)]
    behind = [(0, 0), (1, 1)] if groups > 1 else []
    for i, (g, d) in enumerate(ahead + behind):

        @pl.when(down_ok(g) if d else up_ok(g))
        def _():
            hop(seq, g, d, kv_hbm).start()

        if i == 1:
            hop(seq, mine, 2, kv_hbm).start()

    loads[0].wait()
    for copy in loads[4:]:
        copy.start()

    @pl.loop(0, rows // 32)
    def _(i):
        span = pl.ds(pl.multiple_of(i * 32, 32), 32)
        a = tok[span, :].astype(jnp.float32)
        scale = lax.rsqrt(jnp.mean(a * a, axis=-1, keepdims=True) + 1e-05)
        normed[span, :] = (a * scale * gain[...]).astype(jnp.bfloat16)

    for j, w in enumerate((wk, wv)):
        loads[1 + j].wait()
        res = jnp.dot(normed[...], w[...], preferred_element_type=jnp.float32).astype(jnp.bfloat16)
        for g in range(groups):
            near[g, j] = res[:, g * hd : (g + 1) * hd]

    if pair:
        lend_near.start()

        @pl.when(crossing)
        def _():
            for copy in cross:
                copy.start()

        @pl.when(col == 0)
        def _():
            beside(near.at[mine], True).start()

        @pl.when((col == 1) & (mine == 0))
        def _():
            beside(near.at[0], False).start()

    else:

        @pl.when(seq < n - 1)
        def _():
            shift.start()

    for j in range(4):
        loads[3 + j].wait()
        res = jnp.dot(
            normed[...], wq[:, columns(j)], preferred_element_type=jnp.float32
        ).astype(jnp.bfloat16)
        for k in range(tile // hd):
            q[lax.rem(j + 2 * theirs, 4) * (tile // hd) + k] = res[:, k * hd : (k + 1) * hd]
        if pair and j == 1:
            lend_q.start()

    def reach(t, d):
        r = row + t * (2 * d - 1)
        return r, (r >= 0) & (r < length)

    def relay(t, which):
        for g, d in which:
            r, ok = reach(t, d)

            @pl.when(ok & get_ok(g, d))
            def _():
                s = r * 2 + col
                hop(s, g, 2).wait_recv()

                @pl.when(down_ok(g) if d else up_ok(g))
                def _():
                    hop(s, g, d).start()

                @pl.when(g == mine)
                def _():
                    hop(s, g, 2).start()

    relay(1, ahead)

    factor = math.log2(math.e) / math.sqrt(hd)

    extra = acc.shape[1] - hd

    def fold(sets, keys, values, allowed=None, live=None, some=None):
        heads = [i * per + k for i in sets for k in range(per)]
        old = [(mx[h], acc[h]) for h in heads]
        fresh = []
        ones = jnp.ones((extra, keys.shape[0]), jnp.bfloat16)
        lhs = jnp.concatenate([jnp.transpose(values), ones], axis=0)
        if live is not None:
            lhs = lhs * live

        def score(h):
            queries = q[mine * per + h] if h < per else q2[h - per]
            res = lax.dot_general(
                keys, queries, (((1,), (1,)), ((), ())), preferred_element_type=jnp.float32
            )
            return res if allowed is None else jnp.where(allowed, res, -jnp.inf)

        ahead = score(heads[0])
        for k, (m, a) in enumerate(old):
            scores = ahead
            if k + 1 < len(heads):
                ahead = score(heads[k + 1])
            new = jnp.maximum(m, jnp.max(scores, axis=0, keepdims=True))
            weights = jnp.exp2((scores - new) * factor).astype(jnp.bfloat16)
            if some is not None:
                new = jnp.where(some, new, m)
            decay = jnp.exp2((m - new) * factor)
            a = a * decay + jnp.dot(lhs, weights, preferred_element_type=jnp.float32)
            fresh.append((new, a))
        for h, (m, a) in zip(heads, fresh):
            mx[h], acc[h] = m, a

    shape = (rows, rows)
    u_index = lax.broadcasted_iota(jnp.int32, shape, 0)
    t_index = lax.broadcasted_iota(jnp.int32, shape, 1)
    gap = t_index // BLK - u_index // BLK
    mx[...] = jnp.full(mx.shape, -1e30, jnp.float32)
    acc[...] = jnp.zeros(acc.shape, jnp.float32)

    def spans(i, span, offset):
        allowed = (gap + offset == 0) & (u_index <= t_index)
        for e in range(so.shape[1]):
            step = jnp.where(e < sc[mine], so[mine, e], -1)
            allowed = allowed | ((gap + offset == step) & (step >= 0))
        fold([i], span[0], span[1], allowed)

    spans(0, near.at[mine], 0)
    relay(1, behind)

    slots = kv.shape[3]
    slot_block = lax.broadcasted_iota(jnp.int32, (extra, slots), 1) // BLK
    slot_block = slot_block.astype(jnp.float32)
    entry = lax.broadcasted_iota(jnp.int32, (1, vb.shape[1]), 1)
    for g in range(groups):
        block = vb[g : g + 1, :]
        owner[g] = jnp.where((entry < vc[g]) & (block >= 0), lax.div(block, per_device), -1)

    sets = [0, 1] if pair else [0]

    both = [0, 1] if pair else [0]

    def attend(s, sets):
        held = jnp.where(owner[mine] == s, 1.0, 0.0)
        count = jnp.sum(held, axis=1, keepdims=True)
        live = jnp.where(slot_block < count, 1.0, 0.0).astype(jnp.bfloat16)
        live = jnp.concatenate([live] * (acc.shape[1] // extra), axis=0)
        fold(sets, kv[s, mine, 0], kv[s, mine, 1], live=live, some=count > 0)

    def visit(t, side, wait, sets):
        def one(d, _):
            r, ok = reach(t, d)
            if side is other:
                ok = ok & ((t > 0) | (d == 0))

            @pl.when(ok)
            def _():
                s = r * 2 + side
                if wait:
                    hop(s, mine, 2).wait_recv()
                attend(s, sets)

            return 0

        lax.fori_loop(0, 2, one, 0)

    def first(sets):
        def one(i, _):
            r = row + i - 1

            @pl.when((r >= 0) & (r < length))
            def _():
                attend(r * 2 + col, sets)

            return 0

        lax.fori_loop(0, 3, one, 0)

    own.wait()
    first([0])
    if pair:
        lend_near.wait_recv()

        @pl.when(col == 0)
        def _():
            beside(near2, False).start()

        @pl.when((col == 1) & (mine == 1))
        def _():
            beside(near2, True).start()

    def rounds(t, _):
        @pl.when(t > 1)
        def _():
            visit(t, col, False, both)

        @pl.when(t < length - 1)
        def _():
            relay(t + 1, ahead)

        @pl.when((t == 1) & (seq > 0))
        def _():
            shift.wait_recv()
            spans(0, prev, rows // BLK)

        if pair:

            @pl.when(t == 1)
            def _():
                lend_q.wait_recv()
                first([1])
                spans(1, near2, 0)

        @pl.when(t < length - 1)
        def _():
            relay(t + 1, behind)

        @pl.when(t < length - 1)
        def _():
            visit(t - 1, other, True, both)

        if pair:

            @pl.when((t == 1) & (mate > 0))
            def _():
                beside(near2, False).wait_recv()
                spans(1, prev2, rows // BLK)

        return 0

    lax.fori_loop(1, length, rounds, 0)
    visit(length - 2, other, True, both[-1:])
    visit(length - 1, other, True, both[-1:])

    short = rows // 2

    def settled(h, p):
        span = slice(p * short, (p + 1) * short)
        return jnp.transpose(acc[h, :hd, span] / acc[h, hd : hd + 1, span]).astype(jnp.bfloat16)

    if pair:
        for p in range(2):
            for k in range(per):
                attb[p * short : (p + 1) * short, k * hd : (k + 1) * hd] = settled(per + k, p)
            give(p).start()
        visit(length - 2, other, False, [0])
        visit(length - 1, other, False, [0])
    for p in range(2):
        for k in range(per):
            att[mine, p * short : (p + 1) * short, k * hd : (k + 1) * hd] = settled(k, p)

    loads[7].wait()
    width = part.shape[2]
    across = out.shape[1] // width
    pieces = 2 * across

    def product(target, j):
        start = pl.multiple_of(target * out.shape[1] + j % across * width, width)
        total = None
        for g in range(groups):
            res = jnp.dot(
                att[g, j // across * short : (j // across + 1) * short, :],
                wo[g * att.shape[2] : (g + 1) * att.shape[2], pl.ds(start, width)],
                preferred_element_type=jnp.float32,
            )
            total = res if total is None else total + res
        return total

    def core_copy(i):
        return pltpu.make_async_remote_copy(
            src_ref=core_out.at[i],
            dst_ref=core_in.at[i],
            send_sem=core_send.at[i],
            recv_sem=core_recv.at[i],
            device_id=(core_peer, seq),
            device_id_type=MESH,
        )

    def x_copy(step, j):
        i = (step - 1) * pieces + j
        return pltpu.make_async_remote_copy(
            src_ref=x_out.at[i],
            dst_ref=x_in.at[i],
            send_sem=x_send.at[i],
            recv_sem=x_recv.at[i],
            device_id=(chip_peer(head, step), seq),
            device_id_type=MESH,
        )

    todo = [
        (step, p * across + c)
        for p in range(2)
        for step in range(1, chips + 1)
        for c in range(across)
    ]

    def exchange(i):
        step, j = todo[i]
        core_out[i] = product(chip_peer(core_peer, step), j).astype(jnp.bfloat16)
        core_copy(i).start()
        part[i] = product(chip_peer(head, step), j)

    def combine(i):
        step, j = todo[i]
        core_copy(i).wait_recv()
        both = part[i] + core_in[i].astype(jnp.float32)
        if step < chips:
            x_out[(step - 1) * pieces + j] = both.astype(jnp.bfloat16)
        else:
            part[i] = both

    def forward(i):
        combine(i)
        if todo[i][0] < chips:
            x_copy(*todo[i]).start()

    lag = min(2, len(todo))
    for i in range(len(todo)):
        if pair and i % (len(todo) // 2) == 0:
            p = i // (len(todo) // 2)
            part_rows = pl.ds(p * short, short)
            sided(3 + p, attb.at[part_rows], att.at[theirs, part_rows]).wait_recv()
        exchange(i)
        if i >= lag:
            forward(i - lag)
    for i in range(len(todo) - lag, len(todo)):
        forward(i)
    for j in range(pieces):
        total = part[todo.index((chips, j))]
        for step in range(1, chips):
            x_copy(step, j).wait_recv()
            total = total + x_in[(step - 1) * pieces + j].astype(jnp.float32)
        span = slice(j // across * short, (j // across + 1) * short)
        out[span, j % across * width : (j % across + 1) * width] = total.astype(jnp.bfloat16)
    for i, (step, j) in enumerate(todo):
        core_copy(i).wait_send()
        if step < chips:
            x_copy(step, j).wait_send()

    if pair:
        lend_q.wait_send()
        lend_near.wait_send()

        @pl.when(crossing)
        def _():
            for copy in cross:
                copy.wait_send()

        @pl.when((col == 0) | (mine == 1))
        def _():
            beside(near2, True).wait_send()

        @pl.when((col == 0) | (mine == 0))
        def _():
            beside(near2, False).wait_send()

        for p in range(2):
            give(p).wait_send()

    if not pair:

        @pl.when(seq < n - 1)
        def _():
            shift.wait_send()

    def settle(t, _):
        for g in range(groups):
            for d in range(2):
                r, ok = reach(t, d)
                once = (ok if d else ok & (t > 0)) & ((t == 0) | get_ok(g, d))

                @pl.when(once)
                def _():
                    s = r * 2 + col

                    @pl.when(g == mine)
                    def _():
                        hop(s, g, 2).wait_send()

                    @pl.when(down_ok(g) & ((t == 0) | (d == 1)))
                    def _():
                        hop(s, g, 1).wait_send()

                    @pl.when(up_ok(g) & ((t == 0) | (d == 0)))
                    def _():
                        hop(s, g, 0).wait_send()

        return 0

    lax.fori_loop(0, length, settle, 0)


def local(
    n,
    chips,
    tokens,
    norm_gain,
    w_query,
    w_key,
    w_value,
    w_out,
    cache_keys,
    cache_values,
    vert_blocks,
    vert_count,
    slash_offsets,
    slash_count,
):
    groups, _, hd = cache_keys.shape
    rows, model = tokens.shape
    qcols = w_query.shape[1]
    qheads = qcols // hd
    per = qheads // groups
    out_cols = w_out.shape[1] // (2 * chips)
    slots = VCAP * BLK
    bf16, f32 = jnp.bfloat16, jnp.float32
    smem = pl.BlockSpec(memory_space=pltpu.SMEM)
    vmem = pl.BlockSpec(memory_space=pltpu.VMEM)
    hbm = pl.BlockSpec(memory_space=pl.ANY)
    kv = pl.pallas_call(
        pick_kernel,
        out_shape=jax.ShapeDtypeStruct((groups, 2, slots, hd), bf16),
        in_specs=[smem] * 2 + [hbm] * 2,
        out_specs=vmem,
        scratch_shapes=[
            pltpu.SMEM((groups * 2 * VCAP,), jnp.int32),
            pltpu.SemaphoreType.DMA((groups, 2, VCAP)),
        ],
        compiler_params=pltpu.CompilerParams(vmem_limit_bytes=60 << 20),
        name="pick",
    )(vert_blocks, vert_count, cache_keys, cache_values)
    pieces = 4
    width, short = out_cols // 2, rows // 2
    dma = pltpu.SemaphoreType.DMA
    return pl.pallas_call(
        functools.partial(layer_kernel, n, chips, cache_keys.shape[1] // BLK),
        out_shape=jax.ShapeDtypeStruct((rows, out_cols), bf16),
        in_specs=[smem] * 3 + [vmem] * 2 + [hbm] * 6,
        out_specs=vmem,
        scratch_shapes=[
            pltpu.VMEM((rows, model), bf16),
            pltpu.VMEM((rows, model), bf16),
            pltpu.VMEM(w_query.shape, bf16),
            pltpu.VMEM(w_key.shape, bf16),
            pltpu.VMEM(w_value.shape, bf16),
            pltpu.VMEM(w_out.shape, bf16),
            pltpu.VMEM((n, groups, 2, slots, hd), bf16),
            pltpu.VMEM((groups, 2, rows, hd), bf16),
            pltpu.VMEM((2, rows, hd), bf16),
            pltpu.VMEM((2, rows, hd), bf16),
            pltpu.VMEM((2, rows, hd), bf16),
            pltpu.VMEM((qheads, rows, hd), bf16),
            pltpu.VMEM((per, rows, hd), bf16),
            pltpu.VMEM((2 * per, hd + 16, rows), f32),
            pltpu.VMEM((2 * per, 1, rows), f32),
            pltpu.VMEM((groups, 1, vert_blocks.shape[1]), jnp.int32),
            pltpu.VMEM((groups, rows, qcols // groups), bf16),
            pltpu.VMEM((rows, qcols // groups), bf16),
            pltpu.VMEM((chips * pieces, short, width), bf16),
            pltpu.VMEM((chips * pieces, short, width), bf16),
            pltpu.VMEM(((chips - 1) * pieces, short, width), bf16),
            pltpu.VMEM(((chips - 1) * pieces, short, width), bf16),
            pltpu.VMEM((chips * pieces, short, width), f32),
            dma((8,)),
            dma(()),
            dma((3, n, groups)),
            dma((n, groups)),
            dma(()),
            dma(()),
            dma((8,)),
            dma((5,)),
            dma((chips * pieces,)),
            dma((chips * pieces,)),
            dma(((chips - 1) * pieces,)),
            dma(((chips - 1) * pieces,)),
        ],
        compiler_params=pltpu.CompilerParams(
            collective_id=0, has_side_effects=True, vmem_limit_bytes=60 << 20
        ),
        name="layer",
    )(
        vert_count,
        slash_offsets,
        slash_count,
        vert_blocks,
        norm_gain.reshape(1, model),
        tokens,
        w_query,
        w_key,
        w_value,
        w_out,
        kv,
    )


def solution(mesh):
    return jax.shard_map(
        functools.partial(local, mesh.shape["seq"], mesh.shape["heads"] // 2),
        mesh=mesh,
        in_specs=(
            P("seq", None),
            P(),
            P(None, "heads"),
            P(None, "heads"),
            P(None, "heads"),
            P("heads", None),
            P("heads", "seq", None),
            P("heads", "seq", None),
            P("heads", None),
            P("heads"),
            P("heads", None),
            P("heads"),
        ),
        out_specs=P("seq", "heads"),
        check_vma=False,
    )
```

```python
import functools
import math

import jax
import jax.numpy as jnp
from jax import lax
from jax.experimental import pallas as pl
from jax.experimental.pallas import tpu as pltpu
from jax.sharding import PartitionSpec as P

BLK = 64
VCAP = 8
SMAX = 4
MESH = pl.DeviceIdType.MESH


def pick_kernel(vb, vc, ck, cv, kv, table, sems):
    heads, per_device = ck.shape[0], ck.shape[1] // BLK
    first = lax.axis_index("seq") * per_device
    stride = 2 * VCAP

    def copies(g, r, row):
        return [
            pltpu.make_async_copy(
                src.at[g, pl.ds(row, BLK)], kv.at[g, j, pl.ds(r * BLK, BLK)], sems.at[g, j, r]
            )
            for j, src in enumerate((ck, cv))
        ]

    for g in range(heads):
        count = jnp.int32(0)
        live = vc[g]
        for e in range(vb.shape[1]):
            block = vb[g, e] - first
            table[g * stride + count] = block
            mine = (e < live) & (block >= 0) & (block < per_device)
            count = count + mine.astype(jnp.int32)
        spare = jnp.where(count > 0, table[g * stride], 0)
        for r in range(VCAP):
            block = jnp.where(r < count, table[g * stride + r], spare)
            for copy in copies(g, r, pl.multiple_of(block * BLK, BLK)):
                copy.start()
    for g in range(heads):
        for r in range(VCAP):
            for copy in copies(g, r, 0):
                copy.wait()


def layer_kernel(
    n,
    chips,
    per_device,
    vc,
    so,
    sc,
    vb,
    gain,
    tok_hbm,
    wq_hbm,
    wk_hbm,
    wv_hbm,
    wo_hbm,
    kv_hbm,
    out,
    tok,
    normed,
    wq,
    wk,
    wv,
    wo,
    kv,
    near,
    prev,
    near2,
    prev2,
    q,
    q2,
    acc,
    mx,
    owner,
    att,
    attb,
    core_out,
    core_in,
    x_out,
    x_in,
    part,
    load_sem,
    own_sem,
    send_sem,
    recv_sem,
    near_send,
    near_recv,
    side_send,
    side_recv,
    core_send,
    core_recv,
    x_send,
    x_recv,
):
    head = lax.axis_index("heads")
    seq = lax.axis_index("seq")
    col, row = lax.rem(seq, 2), lax.div(seq, 2)
    other = 1 - col
    length = n // 2
    groups = kv.shape[1]
    hd, rows = q.shape[2], acc.shape[2]
    qheads = q.shape[0]
    per = qheads // groups
    pair = groups == 2 and length % 2 == 0 and length >= 4
    mine = lax.rem(row, 2) if pair else 0
    theirs = 1 - mine if pair else 0
    mate = seq + 2 - 4 * mine

    def up_ok(g):
        return row < length - (2 if pair and g == 0 else 1)

    def down_ok(g):
        return row > (1 if pair and g == 1 else 0)

    def get_ok(g, d):
        if d:
            return row >= (1 if pair and g == 1 else 0)
        return row < length - (1 if pair and g == 0 else 0)
    core_peer = head + 1 - 2 * lax.rem(head, 2)
    span_heads = 2 * chips

    def chip_peer(h, step):
        return lax.rem(h + 2 * step, span_heads)

    tile = wq.shape[1] // 4

    def columns(j):
        return pl.ds(pl.multiple_of(lax.rem(j + 2 * theirs, 4) * tile, tile), tile)

    def sided(i, src, dst):
        return pltpu.make_async_remote_copy(
            src_ref=src,
            dst_ref=dst,
            send_sem=side_send.at[i],
            recv_sem=side_recv.at[i],
            device_id=(head, mate),
            device_id_type=MESH,
        )

    lend_q = sided(0, q.at[pl.ds(theirs * per, per)], q2)
    lend_near = sided(1, near.at[theirs], near2)
    after = jnp.where(seq < n - 1, seq + 1, seq - 1)
    after_group = lax.rem(lax.div(after, 2), 2) if pair else 0
    shift = pltpu.make_async_remote_copy(
        src_ref=near.at[after_group],
        dst_ref=prev,
        send_sem=near_send,
        recv_sem=near_recv,
        device_id=(head, after),
        device_id_type=MESH,
    )
    crossing = (col == 1) & (mine == 1) & (row < length - 1)

    def before(src, own_rows, target, sem):
        return pltpu.make_async_remote_copy(
            src_ref=src,
            dst_ref=prev if own_rows else prev2,
            send_sem=side_send.at[sem],
            recv_sem=near_recv if own_rows else side_recv.at[2],
            device_id=(head, target),
            device_id_type=MESH,
        )

    def beside(src, own_rows):
        return before(src, own_rows, row * 2 + other, 5 if own_rows else 2)

    cross = [
        before(near.at[0], True, jnp.minimum(seq + 1, n - 1), 6),
        before(near.at[groups - 1], False, jnp.minimum(seq + 3, n - 1), 7),
    ]

    def give(p):
        part_rows = pl.ds(p * (rows // 2), rows // 2)
        return sided(3 + p, attb.at[part_rows], att.at[mine, part_rows])

    loads = [
        pltpu.make_async_copy(tok_hbm, tok, load_sem.at[0]),
        pltpu.make_async_copy(wk_hbm, wk, load_sem.at[1]),
        pltpu.make_async_copy(wv_hbm, wv, load_sem.at[2]),
    ]
    for j in range(4):
        cols = columns(j)
        loads.append(pltpu.make_async_copy(wq_hbm.at[:, cols], wq.at[:, cols], load_sem.at[3 + j]))
    loads.append(pltpu.make_async_copy(wo_hbm, wo, load_sem.at[7]))
    own = pltpu.make_async_copy(kv_hbm, kv.at[seq], own_sem)
    own.start()
    for copy in loads[:4]:
        copy.start()

    barrier = pltpu.get_barrier_semaphore()

    def greet(h, s):
        pl.semaphore_signal(barrier, inc=1, device_id=(h, s), device_id_type=MESH)

    greet(core_peer, seq)
    for step in range(1, chips):
        greet(chip_peer(head, step), seq)
    greet(head, row * 2 + other)

    @pl.when(row > 0)
    def _():
        greet(head, seq - 2)

    @pl.when(row < length - 1)
    def _():
        greet(head, seq + 2)

    if pair:
        crossed = (col == 0) & (row > 1)

        @pl.when(crossed)
        def _():
            greet(head, seq - 1 - 2 * mine)

    else:

        @pl.when(seq > 0)
        def _():
            greet(head, seq - 1)

    def flag(c):
        return jnp.where(c, 1, 0)

    pl.semaphore_wait(
        barrier,
        chips
        + 1
        + flag(row > 0)
        + flag(row < length - 1)
        + (2 * flag(crossing) if pair else flag(seq < n - 1)),
    )

    def hop(s, g, way, src=None):
        target = (seq + 2, seq - 2, row * 2 + other)[way]
        return pltpu.make_async_remote_copy(
            src_ref=kv.at[s, g] if src is None else src.at[g],
            dst_ref=kv.at[s, g],
            send_sem=send_sem.at[way, s, g],
            recv_sem=recv_sem.at[s, g],
            device_id=(head, target),
            device_id_type=MESH,
        )

    ahead = [(groups - 1, 0), (0, 1)]
    behind = [(0, 0), (1, 1)] if groups > 1 else []
    for i, (g, d) in enumerate(ahead + behind):

        @pl.when(down_ok(g) if d else up_ok(g))
        def _():
            hop(seq, g, d, kv_hbm).start()

        if i == 1:
            hop(seq, mine, 2, kv_hbm).start()

    loads[0].wait()
    for copy in loads[4:]:
        copy.start()

    @pl.loop(0, rows // 32)
    def _(i):
        span = pl.ds(pl.multiple_of(i * 32, 32), 32)
        a = tok[span, :].astype(jnp.float32)
        scale = lax.rsqrt(jnp.mean(a * a, axis=-1, keepdims=True) + 1e-05)
        normed[span, :] = (a * scale * gain[...]).astype(jnp.bfloat16)

    for j, w in enumerate((wk, wv)):
        loads[1 + j].wait()
        res = jnp.dot(normed[...], w[...], preferred_element_type=jnp.float32).astype(jnp.bfloat16)
        for g in range(groups):
            near[g, j] = res[:, g * hd : (g + 1) * hd]

    if pair:
        lend_near.start()

        @pl.when(crossing)
        def _():
            for copy in cross:
                copy.start()

        @pl.when(col == 0)
        def _():
            beside(near.at[mine], True).start()

        @pl.when((col == 1) & (mine == 0))
        def _():
            beside(near.at[0], False).start()

    else:

        @pl.when(seq < n - 1)
        def _():
            shift.start()

    for j in range(4):
        loads[3 + j].wait()
        res = jnp.dot(
            normed[...], wq[:, columns(j)], preferred_element_type=jnp.float32
        ).astype(jnp.bfloat16)
        for k in range(tile // hd):
            q[lax.rem(j + 2 * theirs, 4) * (tile // hd) + k] = res[:, k * hd : (k + 1) * hd]
        if pair and j == 1:
            lend_q.start()

    def reach(t, d):
        r = row + t * (2 * d - 1)
        return r, (r >= 0) & (r < length)

    def relay(t, which):
        for g, d in which:
            r, ok = reach(t, d)

            @pl.when(ok & get_ok(g, d))
            def _():
                s = r * 2 + col
                hop(s, g, 2).wait_recv()

                @pl.when(down_ok(g) if d else up_ok(g))
                def _():
                    hop(s, g, d).start()

                @pl.when(g == mine)
                def _():
                    hop(s, g, 2).start()

    relay(1, ahead)

    factor = math.log2(math.e) / math.sqrt(hd)

    extra = acc.shape[1] - hd

    def fold(sets, keys, values, allowed=None, live=None, some=None):
        heads = [i * per + k for i in sets for k in range(per)]
        old = [(mx[h], acc[h]) for h in heads]
        fresh = []
        ones = jnp.ones((extra, keys.shape[0]), jnp.bfloat16)
        lhs = jnp.concatenate([jnp.transpose(values), ones], axis=0)
        if live is not None:
            lhs = lhs * live

        def score(h):
            queries = q[mine * per + h] if h < per else q2[h - per]
            res = lax.dot_general(
                keys, queries, (((1,), (1,)), ((), ())), preferred_element_type=jnp.float32
            )
            return res if allowed is None else jnp.where(allowed, res, -jnp.inf)

        ahead = score(heads[0])
        for k, (m, a) in enumerate(old):
            scores = ahead
            if k + 1 < len(heads):
                ahead = score(heads[k + 1])
            new = jnp.maximum(m, jnp.max(scores, axis=0, keepdims=True))
            weights = jnp.exp2((scores - new) * factor).astype(jnp.bfloat16)
            if some is not None:
                new = jnp.where(some, new, m)
            decay = jnp.exp2((m - new) * factor)
            a = a * decay + jnp.dot(lhs, weights, preferred_element_type=jnp.float32)
            fresh.append((new, a))
        for h, (m, a) in zip(heads, fresh):
            mx[h], acc[h] = m, a

    shape = (rows, rows)
    u_index = lax.broadcasted_iota(jnp.int32, shape, 0)
    t_index = lax.broadcasted_iota(jnp.int32, shape, 1)
    gap = t_index // BLK - u_index // BLK
    mx[...] = jnp.full(mx.shape, -1e30, jnp.float32)
    acc[...] = jnp.zeros(acc.shape, jnp.float32)

    def spans(i, span, offset):
        allowed = (gap + offset == 0) & (u_index <= t_index)
        for e in range(so.shape[1]):
            step = jnp.where(e < sc[mine], so[mine, e], -1)
            allowed = allowed | ((gap + offset == step) & (step >= 0))
        fold([i], span[0], span[1], allowed)

    spans(0, near.at[mine], 0)
    relay(1, behind)

    slots = kv.shape[3]
    slot_block = lax.broadcasted_iota(jnp.int32, (extra, slots), 1) // BLK
    slot_block = slot_block.astype(jnp.float32)
    entry = lax.broadcasted_iota(jnp.int32, (1, vb.shape[1]), 1)
    for g in range(groups):
        block = vb[g : g + 1, :]
        owner[g] = jnp.where((entry < vc[g]) & (block >= 0), lax.div(block, per_device), -1)

    sets = [0, 1] if pair else [0]

    both = [0, 1] if pair else [0]

    def attend(s, sets):
        held = jnp.where(owner[mine] == s, 1.0, 0.0)
        count = jnp.sum(held, axis=1, keepdims=True)
        live = jnp.where(slot_block < count, 1.0, 0.0).astype(jnp.bfloat16)
        live = jnp.concatenate([live] * (acc.shape[1] // extra), axis=0)
        fold(sets, kv[s, mine, 0], kv[s, mine, 1], live=live, some=count > 0)

    def visit(t, side, wait, sets):
        def one(d, _):
            r, ok = reach(t, d)
            if side is other:
                ok = ok & ((t > 0) | (d == 0))

            @pl.when(ok)
            def _():
                s = r * 2 + side
                if wait:
                    hop(s, mine, 2).wait_recv()
                attend(s, sets)

            return 0

        lax.fori_loop(0, 2, one, 0)

    def first(sets):
        def one(i, _):
            r = row + i - 1

            @pl.when((r >= 0) & (r < length))
            def _():
                attend(r * 2 + col, sets)

            return 0

        lax.fori_loop(0, 3, one, 0)

    own.wait()
    first([0])
    if pair:
        lend_near.wait_recv()

        @pl.when(col == 0)
        def _():
            beside(near2, False).start()

        @pl.when((col == 1) & (mine == 1))
        def _():
            beside(near2, True).start()

    def rounds(t, _):
        @pl.when((t > 1) & (t < length - 1) if pair else t > 1)
        def _():
            visit(t, col, False, both)

        if pair:

            @pl.when(t == length - 1)
            def _():
                visit(t, col, False, [1])

        @pl.when(t < length - 1)
        def _():
            relay(t + 1, ahead)

        @pl.when((t == 1) & (seq > 0))
        def _():
            shift.wait_recv()
            spans(0, prev, rows // BLK)

        if pair:

            @pl.when(t == 1)
            def _():
                lend_q.wait_recv()
                first([1])
                spans(1, near2, 0)

        @pl.when(t < length - 1)
        def _():
            relay(t + 1, behind)

        @pl.when(t < length - (2 if pair else 1))
        def _():
            visit(t - 1, other, True, both)

        if pair:

            @pl.when(t == length - 2)
            def _():
                visit(t - 1, other, True, [1])

        if pair:

            @pl.when((t == 1) & (mate > 0))
            def _():
                beside(near2, False).wait_recv()
                spans(1, prev2, rows // BLK)

        return 0

    lax.fori_loop(1, length, rounds, 0)
    visit(length - 2, other, True, both[-1:])
    visit(length - 1, other, True, both[-1:])

    short = rows // 2

    def settled(h, p):
        span = slice(p * short, (p + 1) * short)
        return jnp.transpose(acc[h, :hd, span] / acc[h, hd : hd + 1, span]).astype(jnp.bfloat16)

    if pair:
        for p in range(2):
            for k in range(per):
                attb[p * short : (p + 1) * short, k * hd : (k + 1) * hd] = settled(per + k, p)
            give(p).start()
        visit(length - 1, col, False, [0])

        def late(t, _):
            visit(t, other, False, [0])
            return 0

        lax.fori_loop(length - 3, length, late, 0)
    for p in range(2):
        for k in range(per):
            att[mine, p * short : (p + 1) * short, k * hd : (k + 1) * hd] = settled(k, p)

    loads[7].wait()
    width = part.shape[2]
    across = out.shape[1] // width
    pieces = 2 * across

    def product(target, j):
        start = pl.multiple_of(target * out.shape[1] + j % across * width, width)
        total = None
        for g in range(groups):
            res = jnp.dot(
                att[g, j // across * short : (j // across + 1) * short, :],
                wo[g * att.shape[2] : (g + 1) * att.shape[2], pl.ds(start, width)],
                preferred_element_type=jnp.float32,
            )
            total = res if total is None else total + res
        return total

    def core_copy(i):
        return pltpu.make_async_remote_copy(
            src_ref=core_out.at[i],
            dst_ref=core_in.at[i],
            send_sem=core_send.at[i],
            recv_sem=core_recv.at[i],
            device_id=(core_peer, seq),
            device_id_type=MESH,
        )

    def x_copy(step, j):
        i = (step - 1) * pieces + j
        return pltpu.make_async_remote_copy(
            src_ref=x_out.at[i],
            dst_ref=x_in.at[i],
            send_sem=x_send.at[i],
            recv_sem=x_recv.at[i],
            device_id=(chip_peer(head, step), seq),
            device_id_type=MESH,
        )

    todo = [
        (step, p * across + c)
        for p in range(2)
        for step in range(1, chips + 1)
        for c in range(across)
    ]

    def lend_part(i):
        step, j = todo[i]
        core_out[i] = product(chip_peer(core_peer, step), j).astype(jnp.bfloat16)
        core_copy(i).start()

    def keep_part(i):
        step, j = todo[i]
        part[i] = product(chip_peer(head, step), j)

    def combine(i):
        step, j = todo[i]
        core_copy(i).wait_recv()
        both = part[i] + core_in[i].astype(jnp.float32)
        if step < chips:
            x_out[(step - 1) * pieces + j] = both.astype(jnp.bfloat16)
        else:
            part[i] = both

    def forward(i):
        combine(i)
        if todo[i][0] < chips:
            x_copy(*todo[i]).start()

    def arrive(p):
        if pair:
            part_rows = pl.ds(p * short, short)
            sided(3 + p, attb.at[part_rows], att.at[theirs, part_rows]).wait_recv()

    for p in range(2):
        arrive(p)
        base = p * (len(todo) // 2)
        crossing_over = range(base, base + (chips - 1) * across)
        staying = range(base + (chips - 1) * across, base + chips * across)
        for i in crossing_over:
            lend_part(i)
        for i in crossing_over:
            keep_part(i)
            forward(i)
        for i in staying:
            lend_part(i)
    for p in range(2):
        base = p * (len(todo) // 2)
        staying = range(base + (chips - 1) * across, base + chips * across)
        for i in staying:
            keep_part(i)
            forward(i)
    for j in range(pieces):
        total = part[todo.index((chips, j))]
        for step in range(1, chips):
            x_copy(step, j).wait_recv()
            total = total + x_in[(step - 1) * pieces + j].astype(jnp.float32)
        span = slice(j // across * short, (j // across + 1) * short)
        out[span, j % across * width : (j % across + 1) * width] = total.astype(jnp.bfloat16)
    for i, (step, j) in enumerate(todo):
        core_copy(i).wait_send()
        if step < chips:
            x_copy(step, j).wait_send()

    if pair:
        lend_q.wait_send()
        lend_near.wait_send()

        @pl.when(crossing)
        def _():
            for copy in cross:
                copy.wait_send()

        @pl.when((col == 0) | (mine == 1))
        def _():
            beside(near2, True).wait_send()

        @pl.when((col == 0) | (mine == 0))
        def _():
            beside(near2, False).wait_send()

        for p in range(2):
            give(p).wait_send()

    if not pair:

        @pl.when(seq < n - 1)
        def _():
            shift.wait_send()

    def settle(t, _):
        for g in range(groups):
            for d in range(2):
                r, ok = reach(t, d)
                once = (ok if d else ok & (t > 0)) & ((t == 0) | get_ok(g, d))

                @pl.when(once)
                def _():
                    s = r * 2 + col

                    @pl.when(g == mine)
                    def _():
                        hop(s, g, 2).wait_send()

                    @pl.when(down_ok(g) & ((t == 0) | (d == 1)))
                    def _():
                        hop(s, g, 1).wait_send()

                    @pl.when(up_ok(g) & ((t == 0) | (d == 0)))
                    def _():
                        hop(s, g, 0).wait_send()

        return 0

    lax.fori_loop(0, length, settle, 0)


def local(
    n,
    chips,
    tokens,
    norm_gain,
    w_query,
    w_key,
    w_value,
    w_out,
    cache_keys,
    cache_values,
    vert_blocks,
    vert_count,
    slash_offsets,
    slash_count,
):
    groups, _, hd = cache_keys.shape
    rows, model = tokens.shape
    qcols = w_query.shape[1]
    qheads = qcols // hd
    per = qheads // groups
    out_cols = w_out.shape[1] // (2 * chips)
    slots = VCAP * BLK
    bf16, f32 = jnp.bfloat16, jnp.float32
    smem = pl.BlockSpec(memory_space=pltpu.SMEM)
    vmem = pl.BlockSpec(memory_space=pltpu.VMEM)
    hbm = pl.BlockSpec(memory_space=pl.ANY)
    kv = pl.pallas_call(
        pick_kernel,
        out_shape=jax.ShapeDtypeStruct((groups, 2, slots, hd), bf16),
        in_specs=[smem] * 2 + [hbm] * 2,
        out_specs=vmem,
        scratch_shapes=[
            pltpu.SMEM((groups * 2 * VCAP,), jnp.int32),
            pltpu.SemaphoreType.DMA((groups, 2, VCAP)),
        ],
        compiler_params=pltpu.CompilerParams(vmem_limit_bytes=60 << 20),
        name="pick",
    )(vert_blocks, vert_count, cache_keys, cache_values)
    pieces = 4
    width, short = out_cols // 2, rows // 2
    dma = pltpu.SemaphoreType.DMA
    return pl.pallas_call(
        functools.partial(layer_kernel, n, chips, cache_keys.shape[1] // BLK),
        out_shape=jax.ShapeDtypeStruct((rows, out_cols), bf16),
        in_specs=[smem] * 3 + [vmem] * 2 + [hbm] * 6,
        out_specs=vmem,
        scratch_shapes=[
            pltpu.VMEM((rows, model), bf16),
            pltpu.VMEM((rows, model), bf16),
            pltpu.VMEM(w_query.shape, bf16),
            pltpu.VMEM(w_key.shape, bf16),
            pltpu.VMEM(w_value.shape, bf16),
            pltpu.VMEM(w_out.shape, bf16),
            pltpu.VMEM((n, groups, 2, slots, hd), bf16),
            pltpu.VMEM((groups, 2, rows, hd), bf16),
            pltpu.VMEM((2, rows, hd), bf16),
            pltpu.VMEM((2, rows, hd), bf16),
            pltpu.VMEM((2, rows, hd), bf16),
            pltpu.VMEM((qheads, rows, hd), bf16),
            pltpu.VMEM((per, rows, hd), bf16),
            pltpu.VMEM((2 * per, hd + 16, rows), f32),
            pltpu.VMEM((2 * per, 1, rows), f32),
            pltpu.VMEM((groups, 1, vert_blocks.shape[1]), jnp.int32),
            pltpu.VMEM((groups, rows, qcols // groups), bf16),
            pltpu.VMEM((rows, qcols // groups), bf16),
            pltpu.VMEM((chips * pieces, short, width), bf16),
            pltpu.VMEM((chips * pieces, short, width), bf16),
            pltpu.VMEM(((chips - 1) * pieces, short, width), bf16),
            pltpu.VMEM(((chips - 1) * pieces, short, width), bf16),
            pltpu.VMEM((chips * pieces, short, width), f32),
            dma((8,)),
            dma(()),
            dma((3, n, groups)),
            dma((n, groups)),
            dma(()),
            dma(()),
            dma((8,)),
            dma((5,)),
            dma((chips * pieces,)),
            dma((chips * pieces,)),
            dma(((chips - 1) * pieces,)),
            dma(((chips - 1) * pieces,)),
        ],
        compiler_params=pltpu.CompilerParams(
            collective_id=0, has_side_effects=True, vmem_limit_bytes=60 << 20
        ),
        name="layer",
    )(
        vert_count,
        slash_offsets,
        slash_count,
        vert_blocks,
        norm_gain.reshape(1, model),
        tokens,
        w_query,
        w_key,
        w_value,
        w_out,
        kv,
    )


def solution(mesh):
    return jax.shard_map(
        functools.partial(local, mesh.shape["seq"], mesh.shape["heads"] // 2),
        mesh=mesh,
        in_specs=(
            P("seq", None),
            P(),
            P(None, "heads"),
            P(None, "heads"),
            P(None, "heads"),
            P("heads", None),
            P("heads", "seq", None),
            P("heads", "seq", None),
            P("heads", None),
            P("heads"),
            P("heads", None),
            P("heads"),
        ),
        out_specs=P("seq", "heads"),
        check_vma=False,
    )
```

```python
import functools
import math

import jax
import jax.numpy as jnp
from jax import lax
from jax.experimental import pallas as pl
from jax.experimental.pallas import tpu as pltpu
from jax.sharding import PartitionSpec as P

BLK = 64
VCAP = 8
SMAX = 4
MESH = pl.DeviceIdType.MESH


def pick_kernel(vb, vc, ck, cv, kv, table, sems):
    heads, per_device = ck.shape[0], ck.shape[1] // BLK
    first = lax.axis_index("seq") * per_device
    stride = 2 * VCAP

    def copies(g, r, row):
        return [
            pltpu.make_async_copy(
                src.at[g, pl.ds(row, BLK)], kv.at[g, j, pl.ds(r * BLK, BLK)], sems.at[g, j, r]
            )
            for j, src in enumerate((ck, cv))
        ]

    for g in range(heads):
        count = jnp.int32(0)
        live = vc[g]
        for e in range(vb.shape[1]):
            block = vb[g, e] - first
            table[g * stride + count] = block
            mine = (e < live) & (block >= 0) & (block < per_device)
            count = count + mine.astype(jnp.int32)
        spare = jnp.where(count > 0, table[g * stride], 0)
        for r in range(VCAP):
            block = jnp.where(r < count, table[g * stride + r], spare)
            for copy in copies(g, r, pl.multiple_of(block * BLK, BLK)):
                copy.start()
    for g in range(heads):
        for r in range(VCAP):
            for copy in copies(g, r, 0):
                copy.wait()


def layer_kernel(
    n,
    chips,
    per_device,
    vc_hbm,
    so_hbm,
    sc_hbm,
    vb_hbm,
    gain_hbm,
    tok_hbm,
    wq_hbm,
    wk_hbm,
    wv_hbm,
    wo_hbm,
    kv_hbm,
    out,
    vc,
    so,
    sc,
    vb,
    gain,
    tok,
    normed,
    wq,
    wk,
    wv,
    wo,
    kv,
    near,
    prev,
    near2,
    prev2,
    q,
    q2,
    acc,
    mx,
    owner,
    att,
    attb,
    core_out,
    core_in,
    x_out,
    x_in,
    part,
    load_sem,
    own_sem,
    list_sem,
    send_sem,
    recv_sem,
    near_send,
    near_recv,
    side_send,
    side_recv,
    core_send,
    core_recv,
    x_send,
    x_recv,
):
    head = lax.axis_index("heads")
    seq = lax.axis_index("seq")
    col, row = lax.rem(seq, 2), lax.div(seq, 2)
    other = 1 - col
    length = n // 2
    groups = kv.shape[1]
    hd, rows = q.shape[2], acc.shape[2]
    qheads = q.shape[0]
    per = qheads // groups
    pair = groups == 2 and length % 2 == 0 and length >= 4
    mine = lax.rem(row, 2) if pair else 0
    theirs = 1 - mine if pair else 0
    mate = seq + 2 - 4 * mine

    def up_ok(g):
        return row < length - (2 if pair and g == 0 else 1)

    def down_ok(g):
        return row > (1 if pair and g == 1 else 0)

    def get_ok(g, d):
        if d:
            return row >= (1 if pair and g == 1 else 0)
        return row < length - (1 if pair and g == 0 else 0)
    core_peer = head + 1 - 2 * lax.rem(head, 2)
    span_heads = 2 * chips

    def chip_peer(h, step):
        return lax.rem(h + 2 * step, span_heads)

    tile = wq.shape[1] // 4

    def columns(j):
        return pl.ds(pl.multiple_of(lax.rem(j + 2 * theirs, 4) * tile, tile), tile)

    def sided(i, src, dst):
        return pltpu.make_async_remote_copy(
            src_ref=src,
            dst_ref=dst,
            send_sem=side_send.at[i],
            recv_sem=side_recv.at[i],
            device_id=(head, mate),
            device_id_type=MESH,
        )

    lend_q = sided(0, q.at[pl.ds(theirs * per, per)], q2)
    lend_near = sided(1, near.at[theirs], near2)
    after = jnp.where(seq < n - 1, seq + 1, seq - 1)
    after_group = lax.rem(lax.div(after, 2), 2) if pair else 0
    shift = pltpu.make_async_remote_copy(
        src_ref=near.at[after_group],
        dst_ref=prev,
        send_sem=near_send,
        recv_sem=near_recv,
        device_id=(head, after),
        device_id_type=MESH,
    )
    crossing = (col == 1) & (mine == 1) & (row < length - 1)

    def before(src, own_rows, target, sem):
        return pltpu.make_async_remote_copy(
            src_ref=src,
            dst_ref=prev if own_rows else prev2,
            send_sem=side_send.at[sem],
            recv_sem=near_recv if own_rows else side_recv.at[2],
            device_id=(head, target),
            device_id_type=MESH,
        )

    def beside(src, own_rows):
        return before(src, own_rows, row * 2 + other, 5 if own_rows else 2)

    cross = [
        before(near.at[0], True, jnp.minimum(seq + 1, n - 1), 6),
        before(near.at[groups - 1], False, jnp.minimum(seq + 3, n - 1), 7),
    ]

    def give(p):
        part_rows = pl.ds(p * (rows // 2), rows // 2)
        return sided(3 + p, attb.at[part_rows], att.at[mine, part_rows])

    loads = [
        pltpu.make_async_copy(tok_hbm, tok, load_sem.at[0]),
        pltpu.make_async_copy(wk_hbm, wk, load_sem.at[1]),
        pltpu.make_async_copy(wv_hbm, wv, load_sem.at[2]),
    ]
    for j in range(4):
        cols = columns(j)
        loads.append(pltpu.make_async_copy(wq_hbm.at[:, cols], wq.at[:, cols], load_sem.at[3 + j]))
    loads.append(pltpu.make_async_copy(wo_hbm, wo, load_sem.at[7]))
    own = pltpu.make_async_copy(kv_hbm, kv.at[seq], own_sem)
    own.start()
    for copy in loads[:4]:
        copy.start()

    lists = [
        pltpu.make_async_copy(src, dst, list_sem.at[i])
        for i, (src, dst) in enumerate(
            (
                (gain_hbm, gain),
                (vb_hbm, vb),
                (vc_hbm, vc),
                (so_hbm, so),
                (sc_hbm, sc),
            )
        )
    ]
    for copy in lists:
        copy.start()

    barrier = pltpu.get_barrier_semaphore()

    def greet(h, s):
        pl.semaphore_signal(barrier, inc=1, device_id=(h, s), device_id_type=MESH)

    greet(core_peer, seq)
    for step in range(1, chips):
        greet(chip_peer(head, step), seq)
    greet(head, row * 2 + other)

    @pl.when(row > 0)
    def _():
        greet(head, seq - 2)

    @pl.when(row < length - 1)
    def _():
        greet(head, seq + 2)

    if pair:
        crossed = (col == 0) & (row > 1)

        @pl.when(crossed)
        def _():
            greet(head, seq - 1 - 2 * mine)

    else:

        @pl.when(seq > 0)
        def _():
            greet(head, seq - 1)

    def flag(c):
        return jnp.where(c, 1, 0)

    pl.semaphore_wait(
        barrier,
        chips
        + 1
        + flag(row > 0)
        + flag(row < length - 1)
        + (2 * flag(crossing) if pair else flag(seq < n - 1)),
    )

    def hop(s, g, way, src=None):
        target = (seq + 2, seq - 2, row * 2 + other)[way]
        return pltpu.make_async_remote_copy(
            src_ref=kv.at[s, g] if src is None else src.at[g],
            dst_ref=kv.at[s, g],
            send_sem=send_sem.at[way, s, g],
            recv_sem=recv_sem.at[s, g],
            device_id=(head, target),
            device_id_type=MESH,
        )

    ahead = [(groups - 1, 0), (0, 1)]
    behind = [(0, 0), (1, 1)] if groups > 1 else []
    for i, (g, d) in enumerate(ahead + behind):

        @pl.when(down_ok(g) if d else up_ok(g))
        def _():
            hop(seq, g, d, kv_hbm).start()

        if i == 1:
            hop(seq, mine, 2, kv_hbm).start()

    for copy in lists:
        copy.wait()
    loads[0].wait()
    for copy in loads[4:]:
        copy.start()

    @pl.loop(0, rows // 32)
    def _(i):
        span = pl.ds(pl.multiple_of(i * 32, 32), 32)
        a = tok[span, :].astype(jnp.float32)
        scale = lax.rsqrt(jnp.mean(a * a, axis=-1, keepdims=True) + 1e-05)
        normed[span, :] = (a * scale * gain[...]).astype(jnp.bfloat16)

    for j, w in enumerate((wk, wv)):
        loads[1 + j].wait()
        res = jnp.dot(normed[...], w[...], preferred_element_type=jnp.float32).astype(jnp.bfloat16)
        for g in range(groups):
            near[g, j] = res[:, g * hd : (g + 1) * hd]

    if pair:
        lend_near.start()

        @pl.when(crossing)
        def _():
            for copy in cross:
                copy.start()

        @pl.when(col == 0)
        def _():
            beside(near.at[mine], True).start()

        @pl.when((col == 1) & (mine == 0))
        def _():
            beside(near.at[0], False).start()

    else:

        @pl.when(seq < n - 1)
        def _():
            shift.start()

    for j in range(4):
        loads[3 + j].wait()
        res = jnp.dot(
            normed[...], wq[:, columns(j)], preferred_element_type=jnp.float32
        ).astype(jnp.bfloat16)
        for k in range(tile // hd):
            q[lax.rem(j + 2 * theirs, 4) * (tile // hd) + k] = res[:, k * hd : (k + 1) * hd]
        if pair and j == 1:
            lend_q.start()

    def reach(t, d):
        r = row + t * (2 * d - 1)
        return r, (r >= 0) & (r < length)

    def relay(t, which):
        for g, d in which:
            r, ok = reach(t, d)

            @pl.when(ok & get_ok(g, d))
            def _():
                s = r * 2 + col
                hop(s, g, 2).wait_recv()

                @pl.when(down_ok(g) if d else up_ok(g))
                def _():
                    hop(s, g, d).start()

                @pl.when(g == mine)
                def _():
                    hop(s, g, 2).start()

    relay(1, ahead)

    factor = math.log2(math.e) / math.sqrt(hd)

    extra = acc.shape[1] - hd

    def fold(sets, keys, values, allowed=None, live=None, some=None):
        heads = [i * per + k for i in sets for k in range(per)]
        old = [(mx[h], acc[h]) for h in heads]
        fresh = []
        ones = jnp.ones((extra, keys.shape[0]), jnp.bfloat16)
        lhs = jnp.concatenate([jnp.transpose(values), ones], axis=0)
        if live is not None:
            lhs = lhs * live

        def score(h):
            queries = q[mine * per + h] if h < per else q2[h - per]
            res = lax.dot_general(
                keys, queries, (((1,), (1,)), ((), ())), preferred_element_type=jnp.float32
            )
            return res if allowed is None else jnp.where(allowed, res, -jnp.inf)

        ahead = score(heads[0])
        for k, (m, a) in enumerate(old):
            scores = ahead
            if k + 1 < len(heads):
                ahead = score(heads[k + 1])
            new = jnp.maximum(m, jnp.max(scores, axis=0, keepdims=True))
            weights = jnp.exp2((scores - new) * factor).astype(jnp.bfloat16)
            if some is not None:
                new = jnp.where(some, new, m)
            decay = jnp.exp2((m - new) * factor)
            a = a * decay + jnp.dot(lhs, weights, preferred_element_type=jnp.float32)
            fresh.append((new, a))
        for h, (m, a) in zip(heads, fresh):
            mx[h], acc[h] = m, a

    shape = (rows, rows)
    u_index = lax.broadcasted_iota(jnp.int32, shape, 0)
    t_index = lax.broadcasted_iota(jnp.int32, shape, 1)
    gap = t_index // BLK - u_index // BLK
    mx[...] = jnp.full(mx.shape, -1e30, jnp.float32)
    acc[...] = jnp.zeros(acc.shape, jnp.float32)

    def spans(i, span, offset):
        allowed = (gap + offset == 0) & (u_index <= t_index)
        for e in range(so.shape[1]):
            step = jnp.where(e < sc[mine], so[mine, e], -1)
            allowed = allowed | ((gap + offset == step) & (step >= 0))
        fold([i], span[0], span[1], allowed)

    spans(0, near.at[mine], 0)
    relay(1, behind)

    slots = kv.shape[3]
    slot_block = lax.broadcasted_iota(jnp.int32, (extra, slots), 1) // BLK
    slot_block = slot_block.astype(jnp.float32)
    entry = lax.broadcasted_iota(jnp.int32, (1, vb.shape[1]), 1)
    for g in range(groups):
        block = vb[g : g + 1, :]
        owner[g] = jnp.where((entry < vc[g]) & (block >= 0), lax.div(block, per_device), -1)

    sets = [0, 1] if pair else [0]

    both = [0, 1] if pair else [0]

    def attend(s, sets):
        held = jnp.where(owner[mine] == s, 1.0, 0.0)
        count = jnp.sum(held, axis=1, keepdims=True)
        live = jnp.where(slot_block < count, 1.0, 0.0).astype(jnp.bfloat16)
        live = jnp.concatenate([live] * (acc.shape[1] // extra), axis=0)
        fold(sets, kv[s, mine, 0], kv[s, mine, 1], live=live, some=count > 0)

    def visit(t, side, wait, sets):
        def one(d, _):
            r, ok = reach(t, d)
            if side is other:
                ok = ok & ((t > 0) | (d == 0))

            @pl.when(ok)
            def _():
                s = r * 2 + side
                if wait:
                    hop(s, mine, 2).wait_recv()
                attend(s, sets)

            return 0

        lax.fori_loop(0, 2, one, 0)

    def first(sets):
        def one(i, _):
            r = row + i - 1

            @pl.when((r >= 0) & (r < length))
            def _():
                attend(r * 2 + col, sets)

            return 0

        lax.fori_loop(0, 3, one, 0)

    own.wait()
    first([0])
    if pair:
        lend_near.wait_recv()

        @pl.when(col == 0)
        def _():
            beside(near2, False).start()

        @pl.when((col == 1) & (mine == 1))
        def _():
            beside(near2, True).start()

    def rounds(t, _):
        @pl.when((t > 1) & (t < length - 1) if pair else t > 1)
        def _():
            visit(t, col, False, both)

        if pair:

            @pl.when(t == length - 1)
            def _():
                visit(t, col, False, [1])

        @pl.when(t < length - 1)
        def _():
            relay(t + 1, ahead)

        if pair:

            @pl.when(t == 1)
            def _():
                lend_q.wait_recv()
                first([1])
                spans(1, near2, 0)

        @pl.when(t < length - 1)
        def _():
            relay(t + 1, behind)

        @pl.when((t == 1) & (seq > 0))
        def _():
            shift.wait_recv()
            spans(0, prev, rows // BLK)

        @pl.when(t < length - (2 if pair else 1))
        def _():
            visit(t - 1, other, True, both)

        if pair:

            @pl.when(t == length - 2)
            def _():
                visit(t - 1, other, True, [1])

        if pair:

            @pl.when((t == 1) & (mate > 0))
            def _():
                beside(near2, False).wait_recv()
                spans(1, prev2, rows // BLK)

        return 0

    lax.fori_loop(1, length, rounds, 0)
    visit(length - 2, other, True, both[-1:])
    visit(length - 1, other, True, both[-1:])

    short = rows // 2

    def settled(h, p):
        span = slice(p * short, (p + 1) * short)
        return jnp.transpose(acc[h, :hd, span] / acc[h, hd : hd + 1, span]).astype(jnp.bfloat16)

    if pair:
        for p in range(2):
            for k in range(per):
                attb[p * short : (p + 1) * short, k * hd : (k + 1) * hd] = settled(per + k, p)
            give(p).start()
        visit(length - 1, col, False, [0])

        def late(t, _):
            visit(t, other, False, [0])
            return 0

        lax.fori_loop(length - 3, length, late, 0)
    for p in range(2):
        for k in range(per):
            att[mine, p * short : (p + 1) * short, k * hd : (k + 1) * hd] = settled(k, p)

    loads[7].wait()
    width = part.shape[2]
    across = out.shape[1] // width
    pieces = 2 * across

    def product(target, j):
        start = pl.multiple_of(target * out.shape[1] + j % across * width, width)
        total = None
        for g in range(groups):
            res = jnp.dot(
                att[g, j // across * short : (j // across + 1) * short, :],
                wo[g * att.shape[2] : (g + 1) * att.shape[2], pl.ds(start, width)],
                preferred_element_type=jnp.float32,
            )
            total = res if total is None else total + res
        return total

    def core_copy(i):
        return pltpu.make_async_remote_copy(
            src_ref=core_out.at[i],
            dst_ref=core_in.at[i],
            send_sem=core_send.at[i],
            recv_sem=core_recv.at[i],
            device_id=(core_peer, seq),
            device_id_type=MESH,
        )

    def x_copy(step, j):
        i = (step - 1) * pieces + j
        return pltpu.make_async_remote_copy(
            src_ref=x_out.at[i],
            dst_ref=x_in.at[i],
            send_sem=x_send.at[i],
            recv_sem=x_recv.at[i],
            device_id=(chip_peer(head, step), seq),
            device_id_type=MESH,
        )

    todo = [
        (step, p * across + c)
        for p in range(2)
        for step in range(1, chips + 1)
        for c in range(across)
    ]

    def lend_part(i):
        step, j = todo[i]
        core_out[i] = product(chip_peer(core_peer, step), j).astype(jnp.bfloat16)
        core_copy(i).start()

    def keep_part(i):
        step, j = todo[i]
        part[i] = product(chip_peer(head, step), j)

    def combine(i):
        step, j = todo[i]
        core_copy(i).wait_recv()
        both = part[i] + core_in[i].astype(jnp.float32)
        if step < chips:
            x_out[(step - 1) * pieces + j] = both.astype(jnp.bfloat16)
        else:
            part[i] = both

    def forward(i):
        combine(i)
        if todo[i][0] < chips:
            x_copy(*todo[i]).start()

    def arrive(p):
        if pair:
            part_rows = pl.ds(p * short, short)
            sided(3 + p, attb.at[part_rows], att.at[theirs, part_rows]).wait_recv()

    for p in range(2):
        arrive(p)
        base = p * (len(todo) // 2)
        crossing_over = range(base, base + (chips - 1) * across)
        staying = range(base + (chips - 1) * across, base + chips * across)
        for i in crossing_over:
            lend_part(i)
        for i in crossing_over:
            keep_part(i)
            forward(i)
        for i in staying:
            lend_part(i)
    for p in range(2):
        base = p * (len(todo) // 2)
        staying = range(base + (chips - 1) * across, base + chips * across)
        for i in staying:
            keep_part(i)
            forward(i)
    for j in range(pieces):
        total = part[todo.index((chips, j))]
        for step in range(1, chips):
            x_copy(step, j).wait_recv()
            total = total + x_in[(step - 1) * pieces + j].astype(jnp.float32)
        span = slice(j // across * short, (j // across + 1) * short)
        out[span, j % across * width : (j % across + 1) * width] = total.astype(jnp.bfloat16)
    for i, (step, j) in enumerate(todo):
        core_copy(i).wait_send()
        if step < chips:
            x_copy(step, j).wait_send()

    if pair:
        lend_q.wait_send()
        lend_near.wait_send()

        @pl.when(crossing)
        def _():
            for copy in cross:
                copy.wait_send()

        @pl.when((col == 0) | (mine == 1))
        def _():
            beside(near2, True).wait_send()

        @pl.when((col == 0) | (mine == 0))
        def _():
            beside(near2, False).wait_send()

        for p in range(2):
            give(p).wait_send()

    if not pair:

        @pl.when(seq < n - 1)
        def _():
            shift.wait_send()

    def settle(t, _):
        for g in range(groups):
            for d in range(2):
                r, ok = reach(t, d)
                once = (ok if d else ok & (t > 0)) & ((t == 0) | get_ok(g, d))

                @pl.when(once)
                def _():
                    s = r * 2 + col

                    @pl.when(g == mine)
                    def _():
                        hop(s, g, 2).wait_send()

                    @pl.when(down_ok(g) & ((t == 0) | (d == 1)))
                    def _():
                        hop(s, g, 1).wait_send()

                    @pl.when(up_ok(g) & ((t == 0) | (d == 0)))
                    def _():
                        hop(s, g, 0).wait_send()

        return 0

    lax.fori_loop(0, length, settle, 0)


def local(
    n,
    chips,
    tokens,
    norm_gain,
    w_query,
    w_key,
    w_value,
    w_out,
    cache_keys,
    cache_values,
    vert_blocks,
    vert_count,
    slash_offsets,
    slash_count,
):
    groups, _, hd = cache_keys.shape
    rows, model = tokens.shape
    qcols = w_query.shape[1]
    qheads = qcols // hd
    per = qheads // groups
    out_cols = w_out.shape[1] // (2 * chips)
    slots = VCAP * BLK
    bf16, f32 = jnp.bfloat16, jnp.float32
    smem = pl.BlockSpec(memory_space=pltpu.SMEM)
    vmem = pl.BlockSpec(memory_space=pltpu.VMEM)
    hbm = pl.BlockSpec(memory_space=pl.ANY)
    kv = pl.pallas_call(
        pick_kernel,
        out_shape=jax.ShapeDtypeStruct((groups, 2, slots, hd), bf16),
        in_specs=[smem] * 2 + [hbm] * 2,
        out_specs=vmem,
        scratch_shapes=[
            pltpu.SMEM((groups * 2 * VCAP,), jnp.int32),
            pltpu.SemaphoreType.DMA((groups, 2, VCAP)),
        ],
        compiler_params=pltpu.CompilerParams(vmem_limit_bytes=60 << 20),
        name="pick",
    )(vert_blocks, vert_count, cache_keys, cache_values)
    pieces = 4
    width, short = out_cols // 2, rows // 2
    dma = pltpu.SemaphoreType.DMA
    return pl.pallas_call(
        functools.partial(layer_kernel, n, chips, cache_keys.shape[1] // BLK),
        out_shape=jax.ShapeDtypeStruct((rows, out_cols), bf16),
        in_specs=[hbm] * 11,
        out_specs=vmem,
        scratch_shapes=[
            pltpu.SMEM(vert_count.shape, jnp.int32),
            pltpu.SMEM(slash_offsets.shape, jnp.int32),
            pltpu.SMEM(slash_count.shape, jnp.int32),
            pltpu.VMEM(vert_blocks.shape, jnp.int32),
            pltpu.VMEM((1, model), f32),
            pltpu.VMEM((rows, model), bf16),
            pltpu.VMEM((rows, model), bf16),
            pltpu.VMEM(w_query.shape, bf16),
            pltpu.VMEM(w_key.shape, bf16),
            pltpu.VMEM(w_value.shape, bf16),
            pltpu.VMEM(w_out.shape, bf16),
            pltpu.VMEM((n, groups, 2, slots, hd), bf16),
            pltpu.VMEM((groups, 2, rows, hd), bf16),
            pltpu.VMEM((2, rows, hd), bf16),
            pltpu.VMEM((2, rows, hd), bf16),
            pltpu.VMEM((2, rows, hd), bf16),
            pltpu.VMEM((qheads, rows, hd), bf16),
            pltpu.VMEM((per, rows, hd), bf16),
            pltpu.VMEM((2 * per, hd + 16, rows), f32),
            pltpu.VMEM((2 * per, 1, rows), f32),
            pltpu.VMEM((groups, 1, vert_blocks.shape[1]), jnp.int32),
            pltpu.VMEM((groups, rows, qcols // groups), bf16),
            pltpu.VMEM((rows, qcols // groups), bf16),
            pltpu.VMEM((chips * pieces, short, width), bf16),
            pltpu.VMEM((chips * pieces, short, width), bf16),
            pltpu.VMEM(((chips - 1) * pieces, short, width), bf16),
            pltpu.VMEM(((chips - 1) * pieces, short, width), bf16),
            pltpu.VMEM((chips * pieces, short, width), f32),
            dma((8,)),
            dma(()),
            dma((5,)),
            dma((3, n, groups)),
            dma((n, groups)),
            dma(()),
            dma(()),
            dma((8,)),
            dma((5,)),
            dma((chips * pieces,)),
            dma((chips * pieces,)),
            dma(((chips - 1) * pieces,)),
            dma(((chips - 1) * pieces,)),
        ],
        compiler_params=pltpu.CompilerParams(
            collective_id=0, has_side_effects=True, vmem_limit_bytes=60 << 20
        ),
        name="layer",
    )(
        vert_count,
        slash_offsets,
        slash_count,
        vert_blocks,
        norm_gain.reshape(1, model),
        tokens,
        w_query,
        w_key,
        w_value,
        w_out,
        kv,
    )


def solution(mesh):
    return jax.shard_map(
        functools.partial(local, mesh.shape["seq"], mesh.shape["heads"] // 2),
        mesh=mesh,
        in_specs=(
            P("seq", None),
            P(),
            P(None, "heads"),
            P(None, "heads"),
            P(None, "heads"),
            P("heads", None),
            P("heads", "seq", None),
            P("heads", "seq", None),
            P("heads", None),
            P("heads"),
            P("heads", None),
            P("heads"),
        ),
        out_specs=P("seq", "heads"),
        check_vma=False,
    )
```

```python
import functools
import math

import jax
import jax.numpy as jnp
from jax import lax
from jax.experimental import pallas as pl
from jax.experimental.pallas import tpu as pltpu
from jax.sharding import PartitionSpec as P

BLK = 64
VCAP = 8
SMAX = 4
MESH = pl.DeviceIdType.MESH


def pick_kernel(vb, vc, ck, cv, kv, table, sems):
    heads, per_device = ck.shape[0], ck.shape[1] // BLK
    first = lax.axis_index("seq") * per_device
    stride = 2 * VCAP

    def copies(g, r, row):
        return [
            pltpu.make_async_copy(
                src.at[g, pl.ds(row, BLK)], kv.at[g, j, pl.ds(r * BLK, BLK)], sems.at[g, j, r]
            )
            for j, src in enumerate((ck, cv))
        ]

    for g in range(heads):
        count = jnp.int32(0)
        live = vc[g]
        for e in range(vb.shape[1]):
            block = vb[g, e] - first
            table[g * stride + count] = block
            mine = (e < live) & (block >= 0) & (block < per_device)
            count = count + mine.astype(jnp.int32)
        spare = jnp.where(count > 0, table[g * stride], 0)
        for r in range(VCAP):
            block = jnp.where(r < count, table[g * stride + r], spare)
            for copy in copies(g, r, pl.multiple_of(block * BLK, BLK)):
                copy.start()
    for g in range(heads):
        for r in range(VCAP):
            for copy in copies(g, r, 0):
                copy.wait()


def layer_kernel(
    n,
    chips,
    per_device,
    vc_hbm,
    so_hbm,
    sc_hbm,
    vb_hbm,
    gain_hbm,
    tok_hbm,
    wq_hbm,
    wk_hbm,
    wv_hbm,
    wo_hbm,
    kv_hbm,
    out_hbm,
    out,
    vc,
    so,
    sc,
    vb,
    gain,
    tok,
    normed,
    wq,
    wk,
    wv,
    wo,
    kv,
    near,
    prev,
    near2,
    prev2,
    q,
    q2,
    acc,
    mx,
    owner,
    att,
    attb,
    core_out,
    core_in,
    x_out,
    x_in,
    part,
    load_sem,
    own_sem,
    list_sem,
    store_sem,
    send_sem,
    recv_sem,
    near_send,
    near_recv,
    side_send,
    side_recv,
    core_send,
    core_recv,
    x_send,
    x_recv,
):
    head = lax.axis_index("heads")
    seq = lax.axis_index("seq")
    col, row = lax.rem(seq, 2), lax.div(seq, 2)
    other = 1 - col
    length = n // 2
    groups = kv.shape[1]
    hd, rows = q.shape[2], acc.shape[2]
    qheads = q.shape[0]
    per = qheads // groups
    pair = groups == 2 and length % 2 == 0 and length >= 4
    mine = lax.rem(row, 2) if pair else 0
    theirs = 1 - mine if pair else 0
    mate = seq + 2 - 4 * mine

    def up_ok(g):
        return row < length - (2 if pair and g == 0 else 1)

    def down_ok(g):
        return row > (1 if pair and g == 1 else 0)

    def get_ok(g, d):
        if d:
            return row >= (1 if pair and g == 1 else 0)
        return row < length - (1 if pair and g == 0 else 0)
    core_peer = head + 1 - 2 * lax.rem(head, 2)
    span_heads = 2 * chips

    def chip_peer(h, step):
        return lax.rem(h + 2 * step, span_heads)

    tile = wq.shape[1] // 4

    def columns(j):
        return pl.ds(pl.multiple_of(lax.rem(j + 2 * theirs, 4) * tile, tile), tile)

    def sided(i, src, dst):
        return pltpu.make_async_remote_copy(
            src_ref=src,
            dst_ref=dst,
            send_sem=side_send.at[i],
            recv_sem=side_recv.at[i],
            device_id=(head, mate),
            device_id_type=MESH,
        )

    lend_q = sided(0, q.at[pl.ds(theirs * per, per)], q2)
    lend_near = sided(1, near.at[theirs], near2)
    after = jnp.where(seq < n - 1, seq + 1, seq - 1)
    after_group = lax.rem(lax.div(after, 2), 2) if pair else 0
    shift = pltpu.make_async_remote_copy(
        src_ref=near.at[after_group],
        dst_ref=prev,
        send_sem=near_send,
        recv_sem=near_recv,
        device_id=(head, after),
        device_id_type=MESH,
    )
    crossing = (col == 1) & (mine == 1) & (row < length - 1)

    def before(src, own_rows, target, sem):
        return pltpu.make_async_remote_copy(
            src_ref=src,
            dst_ref=prev if own_rows else prev2,
            send_sem=side_send.at[sem],
            recv_sem=near_recv if own_rows else side_recv.at[2],
            device_id=(head, target),
            device_id_type=MESH,
        )

    def beside(src, own_rows):
        return before(src, own_rows, row * 2 + other, 5 if own_rows else 2)

    cross = [
        before(near.at[0], True, jnp.minimum(seq + 1, n - 1), 6),
        before(near.at[groups - 1], False, jnp.minimum(seq + 3, n - 1), 7),
    ]

    def give(p):
        part_rows = pl.ds(p * (rows // 2), rows // 2)
        return sided(3 + p, attb.at[part_rows], att.at[mine, part_rows])

    loads = [
        pltpu.make_async_copy(tok_hbm, tok, load_sem.at[0]),
        pltpu.make_async_copy(wk_hbm, wk, load_sem.at[1]),
        pltpu.make_async_copy(wv_hbm, wv, load_sem.at[2]),
    ]
    for j in range(4):
        cols = columns(j)
        loads.append(pltpu.make_async_copy(wq_hbm.at[:, cols], wq.at[:, cols], load_sem.at[3 + j]))
    loads.append(pltpu.make_async_copy(wo_hbm, wo, load_sem.at[7]))
    own = pltpu.make_async_copy(kv_hbm, kv.at[seq], own_sem)
    own.start()
    for copy in loads[:4]:
        copy.start()

    lists = [
        pltpu.make_async_copy(src, dst, list_sem.at[i])
        for i, (src, dst) in enumerate(
            (
                (gain_hbm, gain),
                (vb_hbm, vb),
                (vc_hbm, vc),
                (so_hbm, so),
                (sc_hbm, sc),
            )
        )
    ]
    for copy in lists:
        copy.start()

    barrier = pltpu.get_barrier_semaphore()

    def greet(h, s):
        pl.semaphore_signal(barrier, inc=1, device_id=(h, s), device_id_type=MESH)

    greet(core_peer, seq)
    for step in range(1, chips):
        greet(chip_peer(head, step), seq)
    greet(head, row * 2 + other)

    @pl.when(row > 0)
    def _():
        greet(head, seq - 2)

    @pl.when(row < length - 1)
    def _():
        greet(head, seq + 2)

    if pair:
        crossed = (col == 0) & (row > 1)

        @pl.when(crossed)
        def _():
            greet(head, seq - 1 - 2 * mine)

    else:

        @pl.when(seq > 0)
        def _():
            greet(head, seq - 1)

    def flag(c):
        return jnp.where(c, 1, 0)

    pl.semaphore_wait(
        barrier,
        chips
        + 1
        + flag(row > 0)
        + flag(row < length - 1)
        + (2 * flag(crossing) if pair else flag(seq < n - 1)),
    )

    def hop(s, g, way, src=None):
        target = (seq + 2, seq - 2, row * 2 + other)[way]
        return pltpu.make_async_remote_copy(
            src_ref=kv.at[s, g] if src is None else src.at[g],
            dst_ref=kv.at[s, g],
            send_sem=send_sem.at[way, s, g],
            recv_sem=recv_sem.at[s, g],
            device_id=(head, target),
            device_id_type=MESH,
        )

    ahead = [(groups - 1, 0), (0, 1)]
    behind = [(0, 0), (1, 1)] if groups > 1 else []
    for i, (g, d) in enumerate(ahead + behind):

        @pl.when(down_ok(g) if d else up_ok(g))
        def _():
            hop(seq, g, d, kv_hbm).start()

        if i == 1:
            hop(seq, mine, 2, kv_hbm).start()

    for copy in lists:
        copy.wait()
    loads[0].wait()
    for copy in loads[4:]:
        copy.start()

    @pl.loop(0, rows // 32)
    def _(i):
        span = pl.ds(pl.multiple_of(i * 32, 32), 32)
        a = tok[span, :].astype(jnp.float32)
        scale = lax.rsqrt(jnp.mean(a * a, axis=-1, keepdims=True) + 1e-05)
        normed[span, :] = (a * scale * gain[...]).astype(jnp.bfloat16)

    for j, w in enumerate((wk, wv)):
        loads[1 + j].wait()
        res = jnp.dot(normed[...], w[...], preferred_element_type=jnp.float32).astype(jnp.bfloat16)
        for g in range(groups):
            near[g, j] = res[:, g * hd : (g + 1) * hd]

    if pair:
        lend_near.start()

        @pl.when(crossing)
        def _():
            for copy in cross:
                copy.start()

        @pl.when(col == 0)
        def _():
            beside(near.at[mine], True).start()

        @pl.when((col == 1) & (mine == 0))
        def _():
            beside(near.at[0], False).start()

    else:

        @pl.when(seq < n - 1)
        def _():
            shift.start()

    for j in range(4):
        loads[3 + j].wait()
        res = jnp.dot(
            normed[...], wq[:, columns(j)], preferred_element_type=jnp.float32
        ).astype(jnp.bfloat16)
        for k in range(tile // hd):
            q[lax.rem(j + 2 * theirs, 4) * (tile // hd) + k] = res[:, k * hd : (k + 1) * hd]
        if pair and j == 1:
            lend_q.start()

    def reach(t, d):
        r = row + t * (2 * d - 1)
        return r, (r >= 0) & (r < length)

    def relay(t, which):
        for g, d in which:
            r, ok = reach(t, d)

            @pl.when(ok & get_ok(g, d))
            def _():
                s = r * 2 + col
                hop(s, g, 2).wait_recv()

                @pl.when(down_ok(g) if d else up_ok(g))
                def _():
                    hop(s, g, d).start()

                @pl.when(g == mine)
                def _():
                    hop(s, g, 2).start()

    relay(1, ahead)

    factor = math.log2(math.e) / math.sqrt(hd)

    extra = acc.shape[1] - hd

    def fold(sets, keys, values, allowed=None, live=None, some=None):
        heads = [i * per + k for i in sets for k in range(per)]
        old = [(mx[h], acc[h]) for h in heads]
        fresh = []
        ones = jnp.ones((extra, keys.shape[0]), jnp.bfloat16)
        lhs = jnp.concatenate([jnp.transpose(values), ones], axis=0)
        if live is not None:
            lhs = lhs * live

        def score(h):
            queries = q[mine * per + h] if h < per else q2[h - per]
            res = lax.dot_general(
                keys, queries, (((1,), (1,)), ((), ())), preferred_element_type=jnp.float32
            )
            return res if allowed is None else jnp.where(allowed, res, -jnp.inf)

        ahead = score(heads[0])
        for k, (m, a) in enumerate(old):
            scores = ahead
            if k + 1 < len(heads):
                ahead = score(heads[k + 1])
            new = jnp.maximum(m, jnp.max(scores, axis=0, keepdims=True))
            weights = jnp.exp2((scores - new) * factor).astype(jnp.bfloat16)
            if some is not None:
                new = jnp.where(some, new, m)
            decay = jnp.exp2((m - new) * factor)
            a = a * decay + jnp.dot(lhs, weights, preferred_element_type=jnp.float32)
            fresh.append((new, a))
        for h, (m, a) in zip(heads, fresh):
            mx[h], acc[h] = m, a

    shape = (rows, rows)
    u_index = lax.broadcasted_iota(jnp.int32, shape, 0)
    t_index = lax.broadcasted_iota(jnp.int32, shape, 1)
    gap = t_index // BLK - u_index // BLK
    mx[...] = jnp.full(mx.shape, -1e30, jnp.float32)
    acc[...] = jnp.zeros(acc.shape, jnp.float32)

    def spans(i, span, offset):
        allowed = (gap + offset == 0) & (u_index <= t_index)
        for e in range(so.shape[1]):
            step = jnp.where(e < sc[mine], so[mine, e], -1)
            allowed = allowed | ((gap + offset == step) & (step >= 0))
        fold([i], span[0], span[1], allowed)

    spans(0, near.at[mine], 0)
    relay(1, behind)

    slots = kv.shape[3]
    slot_block = lax.broadcasted_iota(jnp.int32, (extra, slots), 1) // BLK
    slot_block = slot_block.astype(jnp.float32)
    entry = lax.broadcasted_iota(jnp.int32, (1, vb.shape[1]), 1)
    for g in range(groups):
        block = vb[g : g + 1, :]
        owner[g] = jnp.where((entry < vc[g]) & (block >= 0), lax.div(block, per_device), -1)

    sets = [0, 1] if pair else [0]

    both = [0, 1] if pair else [0]

    def attend(s, sets):
        held = jnp.where(owner[mine] == s, 1.0, 0.0)
        count = jnp.sum(held, axis=1, keepdims=True)
        live = jnp.where(slot_block < count, 1.0, 0.0).astype(jnp.bfloat16)
        live = jnp.concatenate([live] * (acc.shape[1] // extra), axis=0)
        fold(sets, kv[s, mine, 0], kv[s, mine, 1], live=live, some=count > 0)

    def visit(t, side, wait, sets):
        def one(d, _):
            r, ok = reach(t, d)
            if side is other:
                ok = ok & ((t > 0) | (d == 0))

            @pl.when(ok)
            def _():
                s = r * 2 + side
                if wait:
                    hop(s, mine, 2).wait_recv()
                attend(s, sets)

            return 0

        lax.fori_loop(0, 2, one, 0)

    def first(sets):
        def one(i, _):
            r = row + i - 1

            @pl.when((r >= 0) & (r < length))
            def _():
                attend(r * 2 + col, sets)

            return 0

        lax.fori_loop(0, 3, one, 0)

    own.wait()
    first([0])
    if pair:
        lend_near.wait_recv()

        @pl.when(col == 0)
        def _():
            beside(near2, False).start()

        @pl.when((col == 1) & (mine == 1))
        def _():
            beside(near2, True).start()

    def rounds(t, _):
        @pl.when((t > 1) & (t < length - 1) if pair else t > 1)
        def _():
            visit(t, col, False, both)

        if pair:

            @pl.when(t == length - 1)
            def _():
                visit(t, col, False, [1])

        @pl.when(t < length - 1)
        def _():
            relay(t + 1, ahead)

        if pair:

            @pl.when(t == 1)
            def _():
                lend_q.wait_recv()
                first([1])
                spans(1, near2, 0)

        @pl.when(t < length - 1)
        def _():
            relay(t + 1, behind)

        @pl.when((t == 1) & (seq > 0))
        def _():
            shift.wait_recv()
            spans(0, prev, rows // BLK)

        @pl.when(t < length - (2 if pair else 1))
        def _():
            visit(t - 1, other, True, both)

        if pair:

            @pl.when(t == length - 2)
            def _():
                visit(t - 1, other, True, [1])

        if pair:

            @pl.when((t == 1) & (mate > 0))
            def _():
                beside(near2, False).wait_recv()
                spans(1, prev2, rows // BLK)

        return 0

    lax.fori_loop(1, length, rounds, 0)
    visit(length - 2, other, True, both[-1:])
    visit(length - 1, other, True, both[-1:])

    short = rows // 2

    def settled(h, p):
        span = slice(p * short, (p + 1) * short)
        return jnp.transpose(acc[h, :hd, span] / acc[h, hd : hd + 1, span]).astype(jnp.bfloat16)

    if pair:
        for p in range(2):
            for k in range(per):
                attb[p * short : (p + 1) * short, k * hd : (k + 1) * hd] = settled(per + k, p)
            give(p).start()
        visit(length - 1, col, False, [0])

        def late(t, _):
            visit(t, other, False, [0])
            return 0

        lax.fori_loop(length - 3, length, late, 0)
    for p in range(2):
        for k in range(per):
            att[mine, p * short : (p + 1) * short, k * hd : (k + 1) * hd] = settled(k, p)

    loads[7].wait()
    width = part.shape[2]
    across = out.shape[1] // width
    pieces = 2 * across

    def product(target, j):
        start = pl.multiple_of(target * out.shape[1] + j % across * width, width)
        total = None
        for g in range(groups):
            res = jnp.dot(
                att[g, j // across * short : (j // across + 1) * short, :],
                wo[g * att.shape[2] : (g + 1) * att.shape[2], pl.ds(start, width)],
                preferred_element_type=jnp.float32,
            )
            total = res if total is None else total + res
        return total

    def core_copy(i):
        return pltpu.make_async_remote_copy(
            src_ref=core_out.at[i],
            dst_ref=core_in.at[i],
            send_sem=core_send.at[i],
            recv_sem=core_recv.at[i],
            device_id=(core_peer, seq),
            device_id_type=MESH,
        )

    def x_copy(step, j):
        i = (step - 1) * pieces + j
        return pltpu.make_async_remote_copy(
            src_ref=x_out.at[i],
            dst_ref=x_in.at[i],
            send_sem=x_send.at[i],
            recv_sem=x_recv.at[i],
            device_id=(chip_peer(head, step), seq),
            device_id_type=MESH,
        )

    todo = [
        (step, p * across + c)
        for p in range(2)
        for step in range(1, chips + 1)
        for c in range(across)
    ]

    def lend_part(i):
        step, j = todo[i]
        core_out[i] = product(chip_peer(core_peer, step), j).astype(jnp.bfloat16)
        core_copy(i).start()

    def keep_part(i):
        step, j = todo[i]
        part[i] = product(chip_peer(head, step), j)

    def combine(i):
        step, j = todo[i]
        core_copy(i).wait_recv()
        both = part[i] + core_in[i].astype(jnp.float32)
        if step < chips:
            x_out[(step - 1) * pieces + j] = both.astype(jnp.bfloat16)
        else:
            part[i] = both

    def forward(i):
        combine(i)
        if todo[i][0] < chips:
            x_copy(*todo[i]).start()

    def arrive(p):
        if pair:
            part_rows = pl.ds(p * short, short)
            sided(3 + p, attb.at[part_rows], att.at[theirs, part_rows]).wait_recv()

    for p in range(2):
        arrive(p)
        base = p * (len(todo) // 2)
        crossing_over = range(base, base + (chips - 1) * across)
        staying = range(base + (chips - 1) * across, base + chips * across)
        for i in crossing_over:
            lend_part(i)
        for i in crossing_over:
            keep_part(i)
            forward(i)
        for i in staying:
            lend_part(i)
    for p in range(2):
        base = p * (len(todo) // 2)
        staying = range(base + (chips - 1) * across, base + chips * across)
        for i in staying:
            keep_part(i)
            forward(i)
    stores = []
    for j in range(pieces):
        total = part[todo.index((chips, j))]
        for step in range(1, chips):
            x_copy(step, j).wait_recv()
            total = total + x_in[(step - 1) * pieces + j].astype(jnp.float32)
        span = slice(j // across * short, (j // across + 1) * short)
        cols = slice(j % across * width, (j % across + 1) * width)
        out[span, cols] = total.astype(jnp.bfloat16)
        if j % across == across - 1:
            stores.append(
                pltpu.make_async_copy(
                    out.at[pl.ds(j // across * short, short)],
                    out_hbm.at[pl.ds(j // across * short, short)],
                    store_sem.at[j // across],
                )
            )
            stores[-1].start()
    for i, (step, j) in enumerate(todo):
        core_copy(i).wait_send()
        if step < chips:
            x_copy(step, j).wait_send()

    if pair:
        lend_q.wait_send()
        lend_near.wait_send()

        @pl.when(crossing)
        def _():
            for copy in cross:
                copy.wait_send()

        @pl.when((col == 0) | (mine == 1))
        def _():
            beside(near2, True).wait_send()

        @pl.when((col == 0) | (mine == 0))
        def _():
            beside(near2, False).wait_send()

        for p in range(2):
            give(p).wait_send()

    if not pair:

        @pl.when(seq < n - 1)
        def _():
            shift.wait_send()

    def settle(t, _):
        for g in range(groups):
            for d in range(2):
                r, ok = reach(t, d)
                once = (ok if d else ok & (t > 0)) & ((t == 0) | get_ok(g, d))

                @pl.when(once)
                def _():
                    s = r * 2 + col

                    @pl.when(g == mine)
                    def _():
                        hop(s, g, 2).wait_send()

                    @pl.when(down_ok(g) & ((t == 0) | (d == 1)))
                    def _():
                        hop(s, g, 1).wait_send()

                    @pl.when(up_ok(g) & ((t == 0) | (d == 0)))
                    def _():
                        hop(s, g, 0).wait_send()

        return 0

    lax.fori_loop(0, length, settle, 0)
    for copy in stores:
        copy.wait()


def local(
    n,
    chips,
    tokens,
    norm_gain,
    w_query,
    w_key,
    w_value,
    w_out,
    cache_keys,
    cache_values,
    vert_blocks,
    vert_count,
    slash_offsets,
    slash_count,
):
    groups, _, hd = cache_keys.shape
    rows, model = tokens.shape
    qcols = w_query.shape[1]
    qheads = qcols // hd
    per = qheads // groups
    out_cols = w_out.shape[1] // (2 * chips)
    slots = VCAP * BLK
    bf16, f32 = jnp.bfloat16, jnp.float32
    smem = pl.BlockSpec(memory_space=pltpu.SMEM)
    vmem = pl.BlockSpec(memory_space=pltpu.VMEM)
    hbm = pl.BlockSpec(memory_space=pl.ANY)
    kv = pl.pallas_call(
        pick_kernel,
        out_shape=jax.ShapeDtypeStruct((groups, 2, slots, hd), bf16),
        in_specs=[smem] * 2 + [hbm] * 2,
        out_specs=vmem,
        scratch_shapes=[
            pltpu.SMEM((groups * 2 * VCAP,), jnp.int32),
            pltpu.SemaphoreType.DMA((groups, 2, VCAP)),
        ],
        compiler_params=pltpu.CompilerParams(vmem_limit_bytes=60 << 20),
        name="pick",
    )(vert_blocks, vert_count, cache_keys, cache_values)
    pieces = 4
    width, short = out_cols // 2, rows // 2
    dma = pltpu.SemaphoreType.DMA
    return pl.pallas_call(
        functools.partial(layer_kernel, n, chips, cache_keys.shape[1] // BLK),
        out_shape=jax.ShapeDtypeStruct((rows, out_cols), bf16),
        in_specs=[hbm] * 11,
        out_specs=hbm,
        scratch_shapes=[
            pltpu.VMEM((rows, out_cols), bf16),
            pltpu.SMEM(vert_count.shape, jnp.int32),
            pltpu.SMEM(slash_offsets.shape, jnp.int32),
            pltpu.SMEM(slash_count.shape, jnp.int32),
            pltpu.VMEM(vert_blocks.shape, jnp.int32),
            pltpu.VMEM((1, model), f32),
            pltpu.VMEM((rows, model), bf16),
            pltpu.VMEM((rows, model), bf16),
            pltpu.VMEM(w_query.shape, bf16),
            pltpu.VMEM(w_key.shape, bf16),
            pltpu.VMEM(w_value.shape, bf16),
            pltpu.VMEM(w_out.shape, bf16),
            pltpu.VMEM((n, groups, 2, slots, hd), bf16),
            pltpu.VMEM((groups, 2, rows, hd), bf16),
            pltpu.VMEM((2, rows, hd), bf16),
            pltpu.VMEM((2, rows, hd), bf16),
            pltpu.VMEM((2, rows, hd), bf16),
            pltpu.VMEM((qheads, rows, hd), bf16),
            pltpu.VMEM((per, rows, hd), bf16),
            pltpu.VMEM((2 * per, hd + 16, rows), f32),
            pltpu.VMEM((2 * per, 1, rows), f32),
            pltpu.VMEM((groups, 1, vert_blocks.shape[1]), jnp.int32),
            pltpu.VMEM((groups, rows, qcols // groups), bf16),
            pltpu.VMEM((rows, qcols // groups), bf16),
            pltpu.VMEM((chips * pieces, short, width), bf16),
            pltpu.VMEM((chips * pieces, short, width), bf16),
            pltpu.VMEM(((chips - 1) * pieces, short, width), bf16),
            pltpu.VMEM(((chips - 1) * pieces, short, width), bf16),
            pltpu.VMEM((chips * pieces, short, width), f32),
            dma((8,)),
            dma(()),
            dma((5,)),
            dma((2,)),
            dma((3, n, groups)),
            dma((n, groups)),
            dma(()),
            dma(()),
            dma((8,)),
            dma((5,)),
            dma((chips * pieces,)),
            dma((chips * pieces,)),
            dma(((chips - 1) * pieces,)),
            dma(((chips - 1) * pieces,)),
        ],
        compiler_params=pltpu.CompilerParams(
            collective_id=0, has_side_effects=True, vmem_limit_bytes=60 << 20
        ),
        name="layer",
    )(
        vert_count,
        slash_offsets,
        slash_count,
        vert_blocks,
        norm_gain.reshape(1, model),
        tokens,
        w_query,
        w_key,
        w_value,
        w_out,
        kv,
    )


def solution(mesh):
    return jax.shard_map(
        functools.partial(local, mesh.shape["seq"], mesh.shape["heads"] // 2),
        mesh=mesh,
        in_specs=(
            P("seq", None),
            P(),
            P(None, "heads"),
            P(None, "heads"),
            P(None, "heads"),
            P("heads", None),
            P("heads", "seq", None),
            P("heads", "seq", None),
            P("heads", None),
            P("heads"),
            P("heads", None),
            P("heads"),
        ),
        out_specs=P("seq", "heads"),
        check_vma=False,
    )
```
